32 devices in a mesh: comp: 2 (over y), tile: 4 (over x, core), lev: 4 (over z).
Axes of the slice: x: 2, y: 2, z: 4, core: 2. Of those that a mesh axis runs over, the one named last changes fastest.
Arguments:
- thermal_anomaly: float32 [2, 80, 2048], P('comp', 'lev', 'tile'), may hold values from -6 to 6
- right_face_transport_ratio: float32 [2, 80, 2048], P('comp', 'lev', 'tile'), may hold values from -0.45 to 0.45
- species_ratios: float32 [2, 40, 80, 2048], P('comp', None, 'lev', 'tile'), may hold values from 0.1 to 3
- lateral_spreading_number: float32 [2, 80, 2048], P('comp', 'lev', 'tile'), may hold values from 0.05 to 0.2
- depth_physics_operator: float32 [2, 80, 80], P('comp'), may hold values from -1 to 1, as said below
- exchange_weight_table: float32 [2048, 4], P('tile'), may hold values from 0.05 to 0.5
- sky_point_of_entry: int32 [2048, 4], P('tile'), may hold values from 0 to 2047, as said below
- water_indicator: int32 [2048], P('tile'), may hold values 0 or 1
Outputs:
- thermal_anomaly_ending: float32 [2, 80, 2048], P('comp', 'lev', 'tile')
- species_ratios_ending: float32 [2, 40, 80, 2048], P('comp', None, 'lev', 'tile')
The draws below stay inside these ranges and needn't reach their ends.
Inputs may be any that keep to these rules, and one draw needn't show every extreme that they name: The ocean cells of each block of 512 (cells b * 512 to (b + 1) * 512 - 1) take their sources near the matching cells of one atmosphere block p(b), p a permutation of the blocks: sky_point_of_entry[j, k] lies cyclically within 128 cells of p(b) * 512 + (j mod 512). `depth_physics_operator`: each matrix has diagonal entries between 0.5 and 1.
All inputs are finite; a program needn't handle non-finite values. No bound on the sum of `water_indicator` on one device may be relied on, other than what follows from the above.
Results may differ from the reference program's by a relative error of at most 0.0003.
Values sent between devices are 32-bit elements; how exact they have to be, the bound alone decides.
No kernel may reach another device: no remote copies, remote signals or barrier semaphores. Data moves between devices by JAX's collectives and lax.ppermute only.
A program may use at most 64 MiB of HBM per device.

```python
import math
import jax
import jax.numpy as jnp
from jax import lax

CELLS = 512
DEPTH_LAYERS = 80
NTRAC = 40
NFLUX = 4
OVER = 4
DOMAIN_PARTS = 2
PART_POINTS = 2048


def draw_depth_physics_operator(key, part):
    key_diag = jax.random.fold_in(key, 11)
    key_off = jax.random.fold_in(key, 12)
    diagonal = jax.random.uniform(key_diag, (DOMAIN_PARTS, DEPTH_LAYERS), jnp.float32, 0.5, 1.0)
    spread = 0.35 / jnp.sqrt(jnp.float32(DEPTH_LAYERS))
    offside = jax.random.normal(key_off, (DOMAIN_PARTS, DEPTH_LAYERS, DEPTH_LAYERS), jnp.float32) * spread
    offside = jnp.clip(offside, -0.45, 0.45)
    identity = jnp.eye(DEPTH_LAYERS, dtype=jnp.float32)
    return offside * (1.0 - identity) + diagonal[:, :, None] * identity


def draw_sky_point_of_entry(key, part):
    key_perm = jax.random.fold_in(key, 21)
    key_sign = jax.random.fold_in(key, 22)
    key_free = jax.random.fold_in(key, 23)
    blocks = PART_POINTS // CELLS
    reach = CELLS // 4
    block_map = jax.random.permutation(key_perm, blocks).astype(jnp.int32)
    cell_index = jnp.arange(PART_POINTS, dtype=jnp.int32)
    centre = block_map[cell_index // CELLS] * CELLS + cell_index % CELLS
    sign = jax.random.randint(key_sign, (PART_POINTS,), 0, 2).astype(jnp.int32) * 2 - 1
    free_offset = jax.random.randint(key_free, (PART_POINTS,), -reach, reach + 1).astype(jnp.int32)
    offsets = jnp.stack([jnp.zeros((PART_POINTS,), jnp.int32), sign * reach, -sign * reach, free_offset], 1)
    return ((centre[:, None] + offsets) % PART_POINTS).astype(jnp.int32)


def place_ends(values, key, smallest, largest):
    dims = values.shape
    index_at = [jax.random.randint(jax.random.fold_in(key, axis), (), 0, dims[axis]) for axis in range(len(dims))]
    values = values.at[tuple(index_at)].set(smallest)
    longest = dims.index(max(dims))
    index_at[longest] = (index_at[longest] + 1) % dims[longest]
    return values.at[tuple(index_at)].set(largest)


def block_levels(rng, shape, cuts, smallest, high):
    def one(axis_at, parts):
        steps = jax.random.uniform(jax.random.fold_in(jax.random.fold_in(rng, 6), axis_at), (parts,), jnp.float32, smallest / len(cuts), high / len(cuts))
        return jnp.repeat(jnp.exp(steps), shape[axis_at] // parts).reshape((-1,) + (1,) * (len(shape) - axis_at - 1))

    level = one(*cuts[0])
    for cut in cuts[1:]:
        level = level * one(*cut)
    return level


def gaussian(own_key, shape, deviation, limit, split=(), kind=jnp.bfloat16):
    loudness = block_levels(own_key, shape, split, -0.22, 0.18) if split else 1.0
    drawn = jax.random.normal(own_key, shape, jnp.float32) * deviation * loudness
    return jnp.minimum(jnp.maximum(drawn, -limit), limit).astype(kind)


def setup_inputs(seed: int = 0) -> dict:
    arg_keys = jax.random.split(jax.random.key(seed), 9)
    return {
        "thermal_anomaly": gaussian(arg_keys[0], (DOMAIN_PARTS, DEPTH_LAYERS, PART_POINTS), 1.0, 6.0, ((0, 2), (1, 4), (2, 4)), jnp.float32),
        "right_face_transport_ratio": jnp.clip(jax.random.uniform(arg_keys[1], (DOMAIN_PARTS, DEPTH_LAYERS, PART_POINTS), jnp.float32, -0.45, 0.45) * block_levels(arg_keys[1], (DOMAIN_PARTS, DEPTH_LAYERS, PART_POINTS), ((0, 2), (1, 4), (2, 4)), -0.4, 0.0), -0.45, 0.45),
        "species_ratios": jnp.clip(jnp.exp(math.log(3.0) - 3.4011974 * jax.random.uniform(arg_keys[2], (DOMAIN_PARTS, NTRAC, DEPTH_LAYERS, PART_POINTS), jnp.float32) ** block_levels(arg_keys[2], (DOMAIN_PARTS, NTRAC, DEPTH_LAYERS, PART_POINTS), ((0, 2), (2, 4), (3, 4)), -0.2, 0.2)), 0.1, 3.0),
        "lateral_spreading_number": jnp.clip(0.05 + 0.15 * jax.random.uniform(arg_keys[3], (DOMAIN_PARTS, DEPTH_LAYERS, PART_POINTS), jnp.float32) ** block_levels(arg_keys[3], (DOMAIN_PARTS, DEPTH_LAYERS, PART_POINTS), ((0, 2), (1, 4), (2, 4)), -0.2, 0.2), 0.05, 0.2),
        "depth_physics_operator": draw_depth_physics_operator(jax.random.fold_in(arg_keys[8], 71), 0),
        "exchange_weight_table": jnp.clip(jnp.exp(math.log(0.5) - 2.3025851 * jax.random.uniform(arg_keys[5], (PART_POINTS, OVER), jnp.float32) ** block_levels(arg_keys[5], (PART_POINTS, OVER), ((0, 4),), -0.2, 0.2)), 0.05, 0.5),
        "sky_point_of_entry": draw_sky_point_of_entry(jax.random.fold_in(arg_keys[8], 71), 0),
        "water_indicator": place_ends((jax.random.randint(arg_keys[7], (PART_POINTS,), 0, 4) < 3).astype(jnp.int32), jax.random.fold_in(arg_keys[7], 1), 0, 1),
    }


def advect(field, speed):
    speed_left = jnp.roll(speed, 1, -1)
    flux_right = jnp.maximum(speed, 0.0) * field + jnp.minimum(speed, 0.0) * jnp.roll(field, -1, -1)
    flux_left = jnp.maximum(speed_left, 0.0) * jnp.roll(field, 1, -1) + jnp.minimum(speed_left, 0.0) * field
    return -(flux_right - flux_left)


def one_step(thermal_energy, speed, tracer_set, lateral_spreading_number):
    heat_next = thermal_energy + (advect(thermal_energy, speed) + lateral_spreading_number * (jnp.roll(thermal_energy, 1, -1) - 2.0 * thermal_energy + jnp.roll(thermal_energy, -1, -1)))
    tracer_next = tracer_set + advect(tracer_set, speed[None])
    return heat_next, tracer_next


def domain_part_advance(items):
    thermal_energy, speed, tracer_set, lateral_spreading_number, sky_indicator = items
    thermal_energy, tracer_set = one_step(thermal_energy, speed, tracer_set, lateral_spreading_number)
    heat_two, tracer_two = one_step(thermal_energy, speed, tracer_set, lateral_spreading_number)
    thermal_energy = jnp.where(sky_indicator, heat_two, thermal_energy)
    tracer_set = jnp.where(sky_indicator, tracer_two, tracer_set)
    return thermal_energy, tracer_set


def reference(thermal_anomaly, right_face_transport_ratio, species_ratios, lateral_spreading_number, depth_physics_operator, exchange_weight_table, sky_point_of_entry, water_indicator):
    sky_indicator = jnp.arange(DOMAIN_PARTS) < DOMAIN_PARTS // 2
    thermal_energy, species_group = lax.map(domain_part_advance, (thermal_anomaly, right_face_transport_ratio, species_ratios, lateral_spreading_number, sky_indicator))
    blended_profiles = jnp.einsum("sij,sjn->sin", depth_physics_operator, thermal_energy, precision=lax.Precision.HIGHEST)
    surface = jnp.concatenate([blended_profiles[:, 0:1], species_group[:, 0:NFLUX - 1, 0]], 1)
    received = jnp.roll(surface, DOMAIN_PARTS // 2, axis=0)
    picked = received[:, :, sky_point_of_entry]
    remapped = jnp.sum(picked * exchange_weight_table, -1)
    updated = surface + 0.5 * (remapped - surface)
    is_sea = jnp.logical_and(jnp.logical_not(sky_indicator)[:, None, None], (water_indicator == 1)[None, None, :])
    renewed_interface_values = jnp.where(is_sea, updated, surface)
    thermal_anomaly_ending = blended_profiles.at[:, 0].set(renewed_interface_values[:, 0])
    species_ratios_ending = species_group.at[:, 0:NFLUX - 1, 0].set(renewed_interface_values[:, 1:])
    return thermal_anomaly_ending, species_ratios_ending
```

```python
import functools

import jax
import jax.numpy as jnp
from jax import lax
from jax.experimental import pallas as pl
from jax.experimental.pallas import tpu as pltpu
from jax.sharding import PartitionSpec as P

NFLUX = 4
LANES = 128
SUB = 8
REACH = 128

VMEM = pl.BlockSpec(memory_space=pltpu.VMEM)
SMEM = pl.BlockSpec(memory_space=pltpu.SMEM)
ANY = pl.BlockSpec(memory_space=pl.ANY)


def padded_rows(n):
    return -(-n // SUB) * SUB


def peer(i, s, n):
    return i ^ s if n & (n - 1) == 0 else (i + s) % n


def slot_of(me, other, n):
    return me ^ other if n & (n - 1) == 0 else lax.rem(me - other + n, n)


def source_of(me, s, n):
    return me ^ s if n & (n - 1) == 0 else lax.rem(me - s + n, n)


def lane_iota(shape):
    return lax.broadcasted_iota(jnp.int32, shape, len(shape) - 1)


def wide(ref, levels, tiles):
    return jnp.concatenate([ref[pl.ds(t, levels, stride=tiles), :] for t in range(tiles)], axis=1)


def from_left(x, k, halo, place):
    moved = pltpu.roll(x, k, 1)
    edge = pltpu.roll(halo, lax.rem(k - place - 2 + 4 * LANES, LANES), 1)
    head = jnp.where(lane_iota(edge.shape) < k, edge, moved[:, :LANES])
    return jnp.concatenate([head, moved[:, LANES:]], axis=1)


def from_right(x, k, halo, place):
    width = x.shape[1]
    moved = pltpu.roll(x, width - k, 1)
    edge = pltpu.roll(halo, lax.rem(LANES - k - place + 4 * LANES, LANES), 1)
    tail = jnp.where(lane_iota(edge.shape) >= LANES - k, edge, moved[:, width - LANES :])
    return jnp.concatenate([moved[:, : width - LANES], tail], axis=1)


def pack_kernel(levels, tiles, tracers, t_ref, u_ref, n_ref, q_ref, a_ref, b_ref, left, right, sems):
    width = tiles * LANES
    copies = [
        pltpu.make_async_copy(q_ref.at[:, :, pl.ds(0, LANES)], left, sems.at[0]),
        pltpu.make_async_copy(q_ref.at[:, :, pl.ds(width - LANES, LANES)], right, sems.at[1]),
    ]
    for copy in copies:
        copy.start()
    even = lax.rem(lax.axis_index("tile"), 2) == 0
    lane = lane_iota((levels, LANES))

    def small(row, shifts, low):
        t, u, n = [r[pl.ds(row, levels, stride=tiles), :] for r in (t_ref, u_ref, n_ref)]
        u = pltpu.roll(u, shifts[0], 1)
        n = pltpu.roll(n, shifts[1], 1)
        if low:
            return jnp.where(lane < 2, t, jnp.where(lane < 4, u, n))
        return jnp.where(lane >= LANES - 2, t, jnp.where(lane >= LANES - 4, u, n))

    small_left = small(0, (2, 4), True)
    small_right = small(tiles - 1, (LANES - 2, LANES - 4), False)
    a_ref[pl.ds(tracers, levels), :] = jnp.where(even, small_right, small_left)
    b_ref[pl.ds(tracers, levels), :] = jnp.where(even, small_left, small_right)
    for copy in copies:
        copy.wait()
    pair = lane_iota((tracers, LANES)) // 2
    packed_left = left[0]
    packed_right = pltpu.roll(right[0], 2, 1)
    for level in range(1, levels):
        here = pair == level
        packed_left = jnp.where(here, pltpu.roll(left[level], 2 * level, 1), packed_left)
        packed_right = jnp.where(here, pltpu.roll(right[level], 2 * level + 2, 1), packed_right)
    a_ref[pl.ds(0, tracers), :] = jnp.where(even, packed_right, packed_left)
    b_ref[pl.ds(0, tracers), :] = jnp.where(even, packed_left, packed_right)


def heat_kernel(levels, tiles, tracers, sections, t_ref, u_ref, n_ref, a_ref, b_ref, heat_ref, coef_ref):
    even = lax.rem(lax.axis_index("tile"), 2) == 0
    ocean = lax.axis_index("comp") >= sections // 2
    t, u, n = [wide(r, levels, tiles) for r in (t_ref, u_ref, n_ref)]
    got_a = a_ref[pl.ds(tracers, levels), :]
    got_b = b_ref[pl.ds(tracers, levels), :]
    low = jnp.where(even, got_b, got_a)
    high = jnp.where(even, got_a, got_b)
    ul1, ul2 = [from_left(u, k, low, LANES - 4) for k in (1, 2)]
    ur1 = from_right(u, 1, high, 2)
    plus = lambda v: jnp.maximum(v, 0.0)
    minus = lambda v: jnp.minimum(v, 0.0)
    a0, b0, c0 = 1.0 - plus(u) + minus(ul1), plus(ul1), -minus(u)
    am, bm, cm = 1.0 - plus(ul1) + minus(ul2), plus(ul2), -minus(ul1)
    ap, bp, cp = 1.0 - plus(ur1) + minus(u), plus(u), -minus(ur1)

    def composed(a0, b0, c0, am, bm, cm, ap, bp, cp):
        return (
            jnp.where(ocean, a0, a0 * a0 + b0 * cm + c0 * bp),
            jnp.where(ocean, b0, b0 * (a0 + am)),
            jnp.where(ocean, c0, c0 * (a0 + ap)),
            jnp.where(ocean, 0.0, b0 * bm),
            jnp.where(ocean, 0.0, c0 * cp),
        )

    for k, value in enumerate(composed(a0, b0, c0, am, bm, cm, ap, bp, cp)):
        coef_ref[k] = value
    nl = from_left(n, 1, low, LANES - 6)
    nr = from_right(n, 1, high, 4)
    e0, e1, e2, e3, e4 = composed(
        a0 - 2.0 * n, b0 + n, c0 + n, am - 2.0 * nl, bm + nl, cm + nl, ap - 2.0 * nr, bp + nr, cp + nr
    )
    tl1, tl2 = [from_left(t, k, low, LANES - 2) for k in (1, 2)]
    tr1, tr2 = [from_right(t, k, high, 0) for k in (1, 2)]
    heat = e0 * t + e1 * tl1 + e2 * tr1 + e3 * tl2 + e4 * tr2
    for tile in range(tiles):
        heat_ref[pl.ds(tile, levels, stride=tiles), :] = heat[:, tile * LANES : (tile + 1) * LANES]


def tracer_kernel(block, tracers, q_ref, coef_ref, a_ref, b_ref, out_ref, top_ref):
    even = lax.rem(lax.axis_index("tile"), 2) == 0
    got_a = a_ref[pl.ds(0, tracers), :]
    got_b = b_ref[pl.ds(0, tracers), :]
    low = jnp.where(even, got_b, got_a)
    high = jnp.where(even, got_a, got_b)
    for i in range(block):
        level = pl.program_id(0) * block + i
        q = q_ref[i]
        place = 2 * level
        e0, e1, e2, e3, e4 = [coef_ref[k, pl.ds(level, 1), :] for k in range(5)]
        new = (
            e0 * q
            + e1 * from_left(q, 1, low, place)
            + e2 * from_right(q, 1, high, place)
            + e3 * from_left(q, 2, low, place)
            + e4 * from_right(q, 2, high, place)
        )
        out_ref[i] = new
        if i == 0:

            @pl.when(pl.program_id(0) == 0)
            def _():
                top_ref[...] = new[:SUB]


def surface_kernel(levels, tiles, count, m_ref, own_ref, *refs):
    got, (top_ref, mixed_ref, send_ref, whole) = refs[: count - 1], refs[count - 1 :]
    for s, ref in enumerate((own_ref,) + tuple(got)):
        whole[pl.ds(s * levels, levels), :] = wide(ref, levels, tiles)
    mixed = jnp.dot(
        m_ref[...], whole[...], precision=lax.Precision.HIGHEST, preferred_element_type=jnp.float32
    )
    mixed_ref[...] = mixed
    fields = jnp.where(
        lax.broadcasted_iota(jnp.int32, (SUB, tiles * LANES), 0) == 0,
        jnp.broadcast_to(mixed[0:1], (SUB, tiles * LANES)),
        pltpu.roll(top_ref[...], 1, 0),
    )
    for tile in range(tiles):
        send_ref[pl.ds(tile * SUB, SUB), :] = fields[:, tile * LANES : (tile + 1) * LANES]


def final_kernel(
    levels, tiles, count, sections, first_ref, mixed_ref, top_ref, index_ref, weight_ref, water_ref, *refs
):
    got, (q_ref, heat_ref, out_ref, whole, patch, sem) = refs[:count], refs[count:]
    del q_ref
    width = tiles * LANES
    cells = count * width
    here = lax.axis_index("tile")
    sea = jnp.logical_and(
        lax.axis_index("comp") >= sections // 2, lax.axis_index("lev") == 0
    )
    rows = tiles * SUB
    for s in range(count):
        whole[pl.ds(pl.multiple_of(source_of(here, s, count) * rows, rows), rows), :] = got[s][...]
    first = first_ref[0]
    top = top_ref[...]
    mixed = mixed_ref[...]
    first_row = lax.broadcasted_iota(jnp.int32, (SUB, LANES), 0) == 0
    lane = lane_iota((SUB, LANES))
    for tile in range(tiles):
        cut = slice(tile * LANES, (tile + 1) * LANES)
        windows = []
        for q in range(3):
            block = lax.rem(first + tile + q - 1 + count * tiles, count * tiles)
            windows.append(whole[pl.ds(pl.multiple_of(block * SUB, SUB), SUB), :])
        total = jnp.zeros((SUB, LANES), jnp.float32)
        start = first * LANES + tile * LANES - REACH
        for k in range(index_ref.shape[0]):
            index = jnp.broadcast_to(index_ref[k : k + 1, cut], (SUB, LANES))
            weight = jnp.broadcast_to(weight_ref[k : k + 1, cut], (SUB, LANES))
            at = index - start - lane
            at = jnp.where(at < 0, at + cells, at)
            at = jnp.where(at >= cells, at - cells, at) + lane
            inner = jnp.bitwise_and(at, LANES - 1)
            outer = jnp.right_shift(at, 7)
            picks = [jnp.take_along_axis(w, inner, axis=1) for w in windows]
            picked = jnp.where(outer == 0, picks[0], jnp.where(outer == 1, picks[1], picks[2]))
            total = total + picked * weight
        own_heat = jnp.broadcast_to(mixed[0:1, cut], (SUB, LANES))
        surface = jnp.where(first_row, own_heat, pltpu.roll(top[:, cut], 1, 0))
        wet = jnp.logical_and(sea, jnp.broadcast_to(water_ref[0:1, cut], (SUB, LANES)) == 1)
        wet = jnp.logical_and(wet, lax.broadcasted_iota(jnp.int32, (SUB, LANES), 0) < NFLUX)
        renewed = jnp.where(wet, surface + 0.5 * (total - surface), surface)
        heat_ref[pl.ds(tile, levels, stride=tiles), :] = mixed[:, cut]
        heat_ref[pl.ds(tile, 1), :] = renewed[0:1]
        patch[:, cut] = jnp.where(
            lax.broadcasted_iota(jnp.int32, (SUB, LANES), 0) < NFLUX - 1,
            pltpu.roll(renewed, SUB - 1, 0),
            top[:, cut],
        )
    copy = pltpu.make_async_copy(patch, out_ref.at[0, pl.ds(0, SUB), :], sem)
    copy.start()
    copy.wait()


def body(
    sizes,
    thermal_anomaly,
    right_face_transport_ratio,
    species_ratios,
    lateral_spreading_number,
    depth_physics_operator,
    exchange_weight_table,
    sky_point_of_entry,
    water_indicator,
):
    sections, tile_count, lev_count = sizes
    _, levels, width = thermal_anomaly.shape
    tracers = species_ratios.shape[1]
    tiles = width // LANES
    rows = levels * tiles
    f32 = jnp.float32
    shape = jax.ShapeDtypeStruct
    flat = lambda x: x.reshape(rows, LANES)
    t, u, n = flat(thermal_anomaly), flat(right_face_transport_ratio), flat(lateral_spreading_number)
    q = jnp.transpose(species_ratios, (0, 2, 1, 3)).reshape(levels, tracers, width)
    lev = lax.axis_index("lev")

    pack_rows = tracers + padded_rows(levels)
    send_a, send_b = pl.pallas_call(
        functools.partial(pack_kernel, levels, tiles, tracers),
        out_shape=[shape((pack_rows, LANES), f32)] * 2,
        in_specs=[VMEM, VMEM, VMEM, ANY],
        out_specs=[VMEM, VMEM],
        scratch_shapes=[pltpu.VMEM((levels, tracers, LANES), f32)] * 2 + [pltpu.SemaphoreType.DMA((2,))],
        name="pack",
    )(t, u, n, q)
    swap_a = [(i, i ^ 1) for i in range(tile_count)]
    swap_b = [(i, (i + 1) % tile_count if i % 2 else (i - 1) % tile_count) for i in range(tile_count)]
    got_a = lax.ppermute(send_a, "tile", swap_a)
    got_b = lax.ppermute(send_b, "tile", swap_b)

    heat, coef = pl.pallas_call(
        functools.partial(heat_kernel, levels, tiles, tracers, sections),
        out_shape=[shape((rows, LANES), f32), shape((5, levels, width), f32)],
        in_specs=[VMEM] * 5,
        out_specs=[VMEM, VMEM],
        name="heat",
    )(t, u, n, got_a, got_b)

    others = [
        lax.ppermute(heat, "lev", [(i, peer(i, s, lev_count)) for i in range(lev_count)])
        for s in range(1, lev_count)
    ]

    block = 5 if levels % 5 == 0 else 1
    whole = lambda *dims: pl.BlockSpec(dims, lambda i: (0,) * len(dims))
    moved, top = pl.pallas_call(
        functools.partial(tracer_kernel, block, tracers),
        out_shape=[shape((levels, tracers, width), f32), shape((SUB, width), f32)],
        grid=(levels // block,),
        in_specs=[
            pl.BlockSpec((block, tracers, width), lambda i: (i, 0, 0)),
            whole(5, levels, width),
            whole(pack_rows, LANES),
            whole(pack_rows, LANES),
        ],
        out_specs=[pl.BlockSpec((block, tracers, width), lambda i: (i, 0, 0)), whole(SUB, width)],
        cost_estimate=pl.CostEstimate(
            flops=9 * levels * tracers * width, bytes_accessed=8 * levels * tracers * width, transcendentals=0
        ),
        name="tracers",
    )(q, coef, got_a, got_b)

    mine = lax.dynamic_slice_in_dim(depth_physics_operator[0], lev * levels, levels, 0)
    columns = [
        lax.dynamic_slice_in_dim(mine, source_of(lev, s, lev_count) * levels, levels, 1)
        for s in range(lev_count)
    ]
    matrix = jnp.concatenate(columns, axis=1)
    mixed, surface = pl.pallas_call(
        functools.partial(surface_kernel, levels, tiles, lev_count),
        out_shape=[shape((levels, width), f32), shape((tiles * SUB, LANES), f32)],
        in_specs=[VMEM] * (lev_count + 2),
        out_specs=[VMEM, VMEM],
        scratch_shapes=[pltpu.VMEM((levels * lev_count, width), f32)],
        name="surface",
    )(matrix, heat, *others, top)

    half = sections // 2
    place = lambda c, i, l: (c * tile_count + i) * lev_count + l
    got = [
        lax.ppermute(
            surface,
            ("comp", "tile", "lev"),
            [
                (place(c, i, l), place((c + half) % sections, peer(i, s, tile_count), l))
                for c in range(sections)
                for i in range(tile_count)
                for l in range(lev_count)
            ],
        )
        for s in range(tile_count)
    ]

    index = sky_point_of_entry.T
    cells = tile_count * width
    first = ((index[0, 0:1] + REACH) % cells) // width * tiles
    heat_out, q_out = pl.pallas_call(
        functools.partial(final_kernel, levels, tiles, tile_count, sections),
        out_shape=[shape((rows, LANES), f32), shape((levels, tracers, width), f32)],
        in_specs=[SMEM] + [VMEM] * (5 + tile_count) + [ANY],
        out_specs=[VMEM, ANY],
        scratch_shapes=[
            pltpu.VMEM((tile_count * tiles * SUB, LANES), f32),
            pltpu.VMEM((SUB, width), f32),
            pltpu.SemaphoreType.DMA,
        ],
        input_output_aliases={6 + tile_count: 1},
        name="remap",
    )(
        first, mixed, top, index, exchange_weight_table.T, water_indicator.reshape(1, width), *got, moved
    )
    thermal_anomaly_ending = heat_out.reshape(1, levels, width)
    species_ratios_ending = jnp.transpose(q_out.reshape(1, levels, tracers, width), (0, 2, 1, 3))
    return thermal_anomaly_ending, species_ratios_ending


def solution(mesh):
    in_specs = (
        P("comp", "lev", "tile"),
        P("comp", "lev", "tile"),
        P("comp", None, "lev", "tile"),
        P("comp", "lev", "tile"),
        P("comp", None, None),
        P("tile", None),
        P("tile", None),
        P("tile"),
    )
    out_specs = (P("comp", "lev", "tile"), P("comp", None, "lev", "tile"))
    sizes = (mesh.shape["comp"], mesh.shape["tile"], mesh.shape["lev"])
    return jax.shard_map(
        functools.partial(body, sizes), mesh=mesh, in_specs=in_specs, out_specs=out_specs, check_vma=False
    )
```

```python
import functools

import jax
import jax.numpy as jnp
from jax import lax
from jax.experimental import pallas as pl
from jax.experimental.pallas import tpu as pltpu
from jax.sharding import PartitionSpec as P

NFLUX = 4
LANES = 128
SUB = 8
REACH = 128

VMEM = pl.BlockSpec(memory_space=pltpu.VMEM)
SMEM = pl.BlockSpec(memory_space=pltpu.SMEM)
ANY = pl.BlockSpec(memory_space=pl.ANY)
PARAMS = pltpu.CompilerParams(vmem_limit_bytes=8 * 2**20)


def padded_rows(n):
    return -(-n // SUB) * SUB


def peer(i, s, n):
    return i ^ s if n & (n - 1) == 0 else (i + s) % n


def slot_of(me, other, n):
    return me ^ other if n & (n - 1) == 0 else lax.rem(me - other + n, n)


def source_of(me, s, n):
    return me ^ s if n & (n - 1) == 0 else lax.rem(me - s + n, n)


def lane_iota(shape):
    return lax.broadcasted_iota(jnp.int32, shape, len(shape) - 1)


def wide(ref, levels, tiles):
    return jnp.concatenate([ref[pl.ds(t, levels, stride=tiles), :] for t in range(tiles)], axis=1)


def from_left(x, k, halo, place):
    moved = pltpu.roll(x, k, 1)
    edge = pltpu.roll(halo, lax.rem(k - place - 2 + 4 * LANES, LANES), 1)
    head = jnp.where(lane_iota(edge.shape) < k, edge, moved[:, :LANES])
    return jnp.concatenate([head, moved[:, LANES:]], axis=1)


def from_right(x, k, halo, place):
    width = x.shape[1]
    moved = pltpu.roll(x, width - k, 1)
    edge = pltpu.roll(halo, lax.rem(LANES - k - place + 4 * LANES, LANES), 1)
    tail = jnp.where(lane_iota(edge.shape) >= LANES - k, edge, moved[:, width - LANES :])
    return jnp.concatenate([moved[:, : width - LANES], tail], axis=1)


def pack_kernel(levels, tiles, tracers, t_ref, u_ref, n_ref, q_ref, a_ref, b_ref, left, right, sems):
    width = tiles * LANES
    copies = [
        pltpu.make_async_copy(q_ref.at[:, :, pl.ds(0, LANES)], left, sems.at[0]),
        pltpu.make_async_copy(q_ref.at[:, :, pl.ds(width - LANES, LANES)], right, sems.at[1]),
    ]
    for copy in copies:
        copy.start()
    even = lax.rem(lax.axis_index("tile"), 2) == 0
    lane = lane_iota((levels, LANES))

    def small(row, shifts, low):
        t, u, n = [r[pl.ds(row, levels, stride=tiles), :] for r in (t_ref, u_ref, n_ref)]
        u = pltpu.roll(u, shifts[0], 1)
        n = pltpu.roll(n, shifts[1], 1)
        if low:
            return jnp.where(lane < 2, t, jnp.where(lane < 4, u, n))
        return jnp.where(lane >= LANES - 2, t, jnp.where(lane >= LANES - 4, u, n))

    small_left = small(0, (2, 4), True)
    small_right = small(tiles - 1, (LANES - 2, LANES - 4), False)
    a_ref[pl.ds(tracers, levels), :] = jnp.where(even, small_right, small_left)
    b_ref[pl.ds(tracers, levels), :] = jnp.where(even, small_left, small_right)
    for copy in copies:
        copy.wait()
    pair = lane_iota((tracers, LANES)) // 2
    packed_left = left[0]
    packed_right = pltpu.roll(right[0], 2, 1)
    for level in range(1, levels):
        here = pair == level
        packed_left = jnp.where(here, pltpu.roll(left[level], 2 * level, 1), packed_left)
        packed_right = jnp.where(here, pltpu.roll(right[level], 2 * level + 2, 1), packed_right)
    a_ref[pl.ds(0, tracers), :] = jnp.where(even, packed_right, packed_left)
    b_ref[pl.ds(0, tracers), :] = jnp.where(even, packed_left, packed_right)


def heat_kernel(levels, tiles, tracers, sections, t_ref, u_ref, n_ref, a_ref, b_ref, heat_ref, coef_ref):
    even = lax.rem(lax.axis_index("tile"), 2) == 0
    ocean = lax.axis_index("comp") >= sections // 2
    t, u, n = [wide(r, levels, tiles) for r in (t_ref, u_ref, n_ref)]
    got_a = a_ref[pl.ds(tracers, levels), :]
    got_b = b_ref[pl.ds(tracers, levels), :]
    low = jnp.where(even, got_b, got_a)
    high = jnp.where(even, got_a, got_b)
    ul1, ul2 = [from_left(u, k, low, LANES - 4) for k in (1, 2)]
    ur1 = from_right(u, 1, high, 2)
    plus = lambda v: jnp.maximum(v, 0.0)
    minus = lambda v: jnp.minimum(v, 0.0)
    a0, b0, c0 = 1.0 - plus(u) + minus(ul1), plus(ul1), -minus(u)
    am, bm, cm = 1.0 - plus(ul1) + minus(ul2), plus(ul2), -minus(ul1)
    ap, bp, cp = 1.0 - plus(ur1) + minus(u), plus(u), -minus(ur1)

    def composed(a0, b0, c0, am, bm, cm, ap, bp, cp):
        return (
            jnp.where(ocean, a0, a0 * a0 + b0 * cm + c0 * bp),
            jnp.where(ocean, b0, b0 * (a0 + am)),
            jnp.where(ocean, c0, c0 * (a0 + ap)),
            jnp.where(ocean, 0.0, b0 * bm),
            jnp.where(ocean, 0.0, c0 * cp),
        )

    for k, value in enumerate(composed(a0, b0, c0, am, bm, cm, ap, bp, cp)):
        coef_ref[k] = value
    nl = from_left(n, 1, low, LANES - 6)
    nr = from_right(n, 1, high, 4)
    e0, e1, e2, e3, e4 = composed(
        a0 - 2.0 * n, b0 + n, c0 + n, am - 2.0 * nl, bm + nl, cm + nl, ap - 2.0 * nr, bp + nr, cp + nr
    )
    tl1, tl2 = [from_left(t, k, low, LANES - 2) for k in (1, 2)]
    tr1, tr2 = [from_right(t, k, high, 0) for k in (1, 2)]
    heat = e0 * t + e1 * tl1 + e2 * tr1 + e3 * tl2 + e4 * tr2
    for tile in range(tiles):
        heat_ref[pl.ds(tile, levels, stride=tiles), :] = heat[:, tile * LANES : (tile + 1) * LANES]


def tracer_kernel(block, tracers, q_ref, coef_ref, a_ref, b_ref, out_ref, top_ref):
    even = lax.rem(lax.axis_index("tile"), 2) == 0
    got_a = a_ref[pl.ds(0, tracers), :]
    got_b = b_ref[pl.ds(0, tracers), :]
    low = jnp.where(even, got_b, got_a)
    high = jnp.where(even, got_a, got_b)
    for i in range(block):
        level = pl.program_id(0) * block + i
        q = q_ref[i]
        place = 2 * level
        e0, e1, e2, e3, e4 = [coef_ref[k, pl.ds(level, 1), :] for k in range(5)]
        new = (
            e0 * q
            + e1 * from_left(q, 1, low, place)
            + e2 * from_right(q, 1, high, place)
            + e3 * from_left(q, 2, low, place)
            + e4 * from_right(q, 2, high, place)
        )
        out_ref[i] = new
        if i == 0:

            @pl.when(pl.program_id(0) == 0)
            def _():
                top_ref[...] = new[:SUB]


def surface_kernel(levels, tiles, count, m_ref, own_ref, *refs):
    got, (top_ref, mixed_ref, send_ref, whole) = refs[: count - 1], refs[count - 1 :]
    for s, ref in enumerate((own_ref,) + tuple(got)):
        whole[pl.ds(s * levels, levels), :] = wide(ref, levels, tiles)
    mixed = jnp.dot(
        m_ref[...], whole[...], precision=lax.Precision.HIGHEST, preferred_element_type=jnp.float32
    )
    mixed_ref[...] = mixed
    fields = jnp.where(
        lax.broadcasted_iota(jnp.int32, (SUB, tiles * LANES), 0) == 0,
        jnp.broadcast_to(mixed[0:1], (SUB, tiles * LANES)),
        pltpu.roll(top_ref[...], 1, 0),
    )
    for tile in range(tiles):
        send_ref[pl.ds(tile * SUB, SUB), :] = fields[:, tile * LANES : (tile + 1) * LANES]


def final_kernel(
    levels, tiles, count, sections, first_ref, mixed_ref, top_ref, index_ref, weight_ref, water_ref, *refs
):
    got, (q_ref, heat_ref, out_ref, whole, patch, sem) = refs[:count], refs[count:]
    del q_ref
    width = tiles * LANES
    cells = count * width
    here = lax.axis_index("tile")
    sea = jnp.logical_and(
        lax.axis_index("comp") >= sections // 2, lax.axis_index("lev") == 0
    )
    rows = tiles * SUB
    for s in range(count):
        whole[pl.ds(pl.multiple_of(source_of(here, s, count) * rows, rows), rows), :] = got[s][...]
    first = first_ref[0]
    top = top_ref[...]
    mixed = mixed_ref[...]
    first_row = lax.broadcasted_iota(jnp.int32, (SUB, LANES), 0) == 0
    lane = lane_iota((SUB, LANES))
    for tile in range(tiles):
        cut = slice(tile * LANES, (tile + 1) * LANES)
        windows = []
        for q in range(3):
            block = lax.rem(first + tile + q - 1 + count * tiles, count * tiles)
            windows.append(whole[pl.ds(pl.multiple_of(block * SUB, SUB), SUB), :])
        total = jnp.zeros((SUB, LANES), jnp.float32)
        start = first * LANES + tile * LANES - REACH
        for k in range(index_ref.shape[0]):
            index = jnp.broadcast_to(index_ref[k : k + 1, cut], (SUB, LANES))
            weight = jnp.broadcast_to(weight_ref[k : k + 1, cut], (SUB, LANES))
            at = index - start - lane
            at = jnp.where(at < 0, at + cells, at)
            at = jnp.where(at >= cells, at - cells, at) + lane
            inner = jnp.bitwise_and(at, LANES - 1)
            outer = jnp.right_shift(at, 7)
            picks = [jnp.take_along_axis(w, inner, axis=1) for w in windows]
            picked = jnp.where(outer == 0, picks[0], jnp.where(outer == 1, picks[1], picks[2]))
            total = total + picked * weight
        own_heat = jnp.broadcast_to(mixed[0:1, cut], (SUB, LANES))
        surface = jnp.where(first_row, own_heat, pltpu.roll(top[:, cut], 1, 0))
        wet = jnp.logical_and(sea, jnp.broadcast_to(water_ref[0:1, cut], (SUB, LANES)) == 1)
        wet = jnp.logical_and(wet, lax.broadcasted_iota(jnp.int32, (SUB, LANES), 0) < NFLUX)
        renewed = jnp.where(wet, surface + 0.5 * (total - surface), surface)
        heat_ref[pl.ds(tile, levels, stride=tiles), :] = mixed[:, cut]
        heat_ref[pl.ds(tile, 1), :] = renewed[0:1]
        patch[:, cut] = jnp.where(
            lax.broadcasted_iota(jnp.int32, (SUB, LANES), 0) < NFLUX - 1,
            pltpu.roll(renewed, SUB - 1, 0),
            top[:, cut],
        )
    copy = pltpu.make_async_copy(patch, out_ref.at[0, pl.ds(0, SUB), :], sem)
    copy.start()
    copy.wait()


def body(
    sizes,
    thermal_anomaly,
    right_face_transport_ratio,
    species_ratios,
    lateral_spreading_number,
    depth_physics_operator,
    exchange_weight_table,
    sky_point_of_entry,
    water_indicator,
):
    sections, tile_count, lev_count = sizes
    _, levels, width = thermal_anomaly.shape
    tracers = species_ratios.shape[1]
    tiles = width // LANES
    rows = levels * tiles
    f32 = jnp.float32
    shape = jax.ShapeDtypeStruct
    flat = lambda x: x.reshape(rows, LANES)
    t, u, n = flat(thermal_anomaly), flat(right_face_transport_ratio), flat(lateral_spreading_number)
    q = jnp.transpose(species_ratios, (0, 2, 1, 3)).reshape(levels, tracers, width)
    lev = lax.axis_index("lev")

    pack_rows = tracers + padded_rows(levels)
    send_a, send_b = pl.pallas_call(
        functools.partial(pack_kernel, levels, tiles, tracers),
        out_shape=[shape((pack_rows, LANES), f32)] * 2,
        in_specs=[VMEM, VMEM, VMEM, ANY],
        out_specs=[VMEM, VMEM],
        scratch_shapes=[pltpu.VMEM((levels, tracers, LANES), f32)] * 2 + [pltpu.SemaphoreType.DMA((2,))],
        compiler_params=PARAMS,
        name="pack",
    )(t, u, n, q)
    swap_a = [(i, i ^ 1) for i in range(tile_count)]
    swap_b = [(i, (i + 1) % tile_count if i % 2 else (i - 1) % tile_count) for i in range(tile_count)]
    got_a = lax.ppermute(send_a, "tile", swap_a)
    got_b = lax.ppermute(send_b, "tile", swap_b)

    heat, coef = pl.pallas_call(
        functools.partial(heat_kernel, levels, tiles, tracers, sections),
        out_shape=[shape((rows, LANES), f32), shape((5, levels, width), f32)],
        in_specs=[VMEM] * 5,
        out_specs=[VMEM, VMEM],
        compiler_params=PARAMS,
        name="heat",
    )(t, u, n, got_a, got_b)

    others = [
        lax.ppermute(heat, "lev", [(i, peer(i, s, lev_count)) for i in range(lev_count)])
        for s in range(1, lev_count)
    ]

    block = 5 if levels % 5 == 0 else 1
    whole = lambda *dims: pl.BlockSpec(dims, lambda i: (0,) * len(dims))
    moved, top = pl.pallas_call(
        functools.partial(tracer_kernel, block, tracers),
        out_shape=[shape((levels, tracers, width), f32), shape((SUB, width), f32)],
        grid=(levels // block,),
        in_specs=[
            pl.BlockSpec((block, tracers, width), lambda i: (i, 0, 0)),
            whole(5, levels, width),
            whole(pack_rows, LANES),
            whole(pack_rows, LANES),
        ],
        out_specs=[pl.BlockSpec((block, tracers, width), lambda i: (i, 0, 0)), whole(SUB, width)],
        cost_estimate=pl.CostEstimate(
            flops=9 * levels * tracers * width, bytes_accessed=8 * levels * tracers * width, transcendentals=0
        ),
        compiler_params=PARAMS,
        name="tracers",
    )(q, coef, got_a, got_b)

    mine = lax.dynamic_slice_in_dim(depth_physics_operator[0], lev * levels, levels, 0)
    columns = [
        lax.dynamic_slice_in_dim(mine, source_of(lev, s, lev_count) * levels, levels, 1)
        for s in range(lev_count)
    ]
    matrix = jnp.concatenate(columns, axis=1)
    mixed, surface = pl.pallas_call(
        functools.partial(surface_kernel, levels, tiles, lev_count),
        out_shape=[shape((levels, width), f32), shape((tiles * SUB, LANES), f32)],
        in_specs=[VMEM] * (lev_count + 2),
        out_specs=[VMEM, VMEM],
        scratch_shapes=[pltpu.VMEM((levels * lev_count, width), f32)],
        compiler_params=PARAMS,
        name="surface",
    )(matrix, heat, *others, top)

    half = sections // 2
    place = lambda c, i, l: (c * tile_count + i) * lev_count + l
    got = [
        lax.ppermute(
            surface,
            ("comp", "tile", "lev"),
            [
                (place(c, i, l), place((c + half) % sections, peer(i, s, tile_count), l))
                for c in range(sections)
                for i in range(tile_count)
                for l in range(lev_count)
            ],
        )
        for s in range(tile_count)
    ]

    index = sky_point_of_entry.T
    cells = tile_count * width
    first = ((index[0, 0:1] + REACH) % cells) // width * tiles
    heat_out, q_out = pl.pallas_call(
        functools.partial(final_kernel, levels, tiles, tile_count, sections),
        out_shape=[shape((rows, LANES), f32), shape((levels, tracers, width), f32)],
        in_specs=[SMEM] + [VMEM] * (5 + tile_count) + [ANY],
        out_specs=[VMEM, ANY],
        scratch_shapes=[
            pltpu.VMEM((tile_count * tiles * SUB, LANES), f32),
            pltpu.VMEM((SUB, width), f32),
            pltpu.SemaphoreType.DMA,
        ],
        input_output_aliases={6 + tile_count: 1},
        compiler_params=PARAMS,
        name="remap",
    )(
        first, mixed, top, index, exchange_weight_table.T, water_indicator.reshape(1, width), *got, moved
    )
    thermal_anomaly_ending = heat_out.reshape(1, levels, width)
    species_ratios_ending = jnp.transpose(q_out.reshape(1, levels, tracers, width), (0, 2, 1, 3))
    return thermal_anomaly_ending, species_ratios_ending


def solution(mesh):
    in_specs = (
        P("comp", "lev", "tile"),
        P("comp", "lev", "tile"),
        P("comp", None, "lev", "tile"),
        P("comp", "lev", "tile"),
        P("comp", None, None),
        P("tile", None),
        P("tile", None),
        P("tile"),
    )
    out_specs = (P("comp", "lev", "tile"), P("comp", None, "lev", "tile"))
    sizes = (mesh.shape["comp"], mesh.shape["tile"], mesh.shape["lev"])
    return jax.shard_map(
        functools.partial(body, sizes), mesh=mesh, in_specs=in_specs, out_specs=out_specs, check_vma=False
    )
```

```python
import functools

import jax
import jax.numpy as jnp
from jax import lax
from jax.experimental import pallas as pl
from jax.experimental.pallas import tpu as pltpu
from jax.sharding import PartitionSpec as P

NFLUX = 4
LANES = 128
SUB = 8
REACH = 128

VMEM = pl.BlockSpec(memory_space=pltpu.VMEM)
SMEM = pl.BlockSpec(memory_space=pltpu.SMEM)
HBM = pl.BlockSpec(memory_space=pltpu.HBM)
PARAMS = pltpu.CompilerParams(vmem_limit_bytes=8 * 2**20)


def padded_rows(n):
    return -(-n // SUB) * SUB


def peer(i, s, n):
    return i ^ s if n & (n - 1) == 0 else (i + s) % n


def slot_of(me, other, n):
    return me ^ other if n & (n - 1) == 0 else lax.rem(me - other + n, n)


def source_of(me, s, n):
    return me ^ s if n & (n - 1) == 0 else lax.rem(me - s + n, n)


def lane_iota(shape):
    return lax.broadcasted_iota(jnp.int32, shape, len(shape) - 1)


def wide(ref, levels, tiles):
    return jnp.concatenate([ref[pl.ds(t, levels, stride=tiles), :] for t in range(tiles)], axis=1)


def from_left(x, k, halo, place):
    moved = pltpu.roll(x, k, 1)
    edge = pltpu.roll(halo, (k - place - 2) % LANES, 1)
    head = jnp.where(lane_iota(edge.shape) < k, edge, moved[:, :LANES])
    return jnp.concatenate([head, moved[:, LANES:]], axis=1)


def from_right(x, k, halo, place):
    width = x.shape[1]
    moved = pltpu.roll(x, width - k, 1)
    edge = pltpu.roll(halo, (-k - place) % LANES, 1)
    tail = jnp.where(lane_iota(edge.shape) >= LANES - k, edge, moved[:, width - LANES :])
    return jnp.concatenate([moved[:, : width - LANES], tail], axis=1)


def pack_kernel(
    levels, tiles, tracers, group, t_hbm, u_hbm, n_hbm, q_hbm, a_ref, b_ref, t_ref, u_ref, n_ref, left, right, sems
):
    width = tiles * LANES
    flats = [
        pltpu.make_async_copy(source, target, sems.at[0, i])
        for i, (source, target) in enumerate(((t_hbm, t_ref), (u_hbm, u_ref), (n_hbm, n_ref)))
    ]
    chunks = []
    for g in range(levels // group):
        cut = pl.ds(g * group, group)
        chunks.append(
            [
                pltpu.make_async_copy(q_hbm.at[cut, :, pl.ds(0, LANES)], left.at[cut], sems.at[1, g]),
                pltpu.make_async_copy(q_hbm.at[cut, :, pl.ds(width - LANES, LANES)], right.at[cut], sems.at[2, g]),
            ]
        )
    for copy in flats:
        copy.start()
    for chunk in chunks:
        for copy in chunk:
            copy.start()
    even = lax.rem(lax.axis_index("tile"), 2) == 0
    lane = lane_iota((levels, LANES))

    def small(row, shifts, low):
        t, u, n = [r[pl.ds(row, levels, stride=tiles), :] for r in (t_ref, u_ref, n_ref)]
        u = pltpu.roll(u, shifts[0], 1)
        n = pltpu.roll(n, shifts[1], 1)
        if low:
            return jnp.where(lane < 2, t, jnp.where(lane < 4, u, n))
        return jnp.where(lane >= LANES - 2, t, jnp.where(lane >= LANES - 4, u, n))

    for copy in flats:
        copy.wait()
    small_left = small(0, (2, 4), True)
    small_right = small(tiles - 1, (LANES - 2, LANES - 4), False)
    a_ref[pl.ds(tracers, levels), :] = jnp.where(even, small_right, small_left)
    b_ref[pl.ds(tracers, levels), :] = jnp.where(even, small_left, small_right)
    pair = lane_iota((tracers, LANES)) // 2
    packed_left = packed_right = jnp.zeros((tracers, LANES), jnp.float32)
    for g, chunk in enumerate(chunks):
        for copy in chunk:
            copy.wait()
        for level in range(g * group, (g + 1) * group):
            here = pair == level
            packed_left = jnp.where(here, pltpu.roll(left[level], 2 * level, 1), packed_left)
            packed_right = jnp.where(here, pltpu.roll(right[level], (2 * level + 2) % LANES, 1), packed_right)
    a_ref[pl.ds(0, tracers), :] = jnp.where(even, packed_right, packed_left)
    b_ref[pl.ds(0, tracers), :] = jnp.where(even, packed_left, packed_right)


def heat_kernel(levels, tiles, tracers, sections, t_ref, u_ref, n_ref, a_ref, b_ref, heat_ref, coef_ref):
    even = lax.rem(lax.axis_index("tile"), 2) == 0
    ocean = lax.axis_index("comp") >= sections // 2
    t, u, n = [wide(r, levels, tiles) for r in (t_ref, u_ref, n_ref)]
    got_a = a_ref[pl.ds(tracers, levels), :]
    got_b = b_ref[pl.ds(tracers, levels), :]
    low = jnp.where(even, got_b, got_a)
    high = jnp.where(even, got_a, got_b)
    ul1, ul2 = [from_left(u, k, low, LANES - 4) for k in (1, 2)]
    ur1 = from_right(u, 1, high, 2)
    plus = lambda v: jnp.maximum(v, 0.0)
    minus = lambda v: jnp.minimum(v, 0.0)
    a0, b0, c0 = 1.0 - plus(u) + minus(ul1), plus(ul1), -minus(u)
    am, bm, cm = 1.0 - plus(ul1) + minus(ul2), plus(ul2), -minus(ul1)
    ap, bp, cp = 1.0 - plus(ur1) + minus(u), plus(u), -minus(ur1)

    def composed(a0, b0, c0, am, bm, cm, ap, bp, cp):
        return (
            jnp.where(ocean, a0, a0 * a0 + b0 * cm + c0 * bp),
            jnp.where(ocean, b0, b0 * (a0 + am)),
            jnp.where(ocean, c0, c0 * (a0 + ap)),
            jnp.where(ocean, 0.0, b0 * bm),
            jnp.where(ocean, 0.0, c0 * cp),
        )

    for k, value in enumerate(composed(a0, b0, c0, am, bm, cm, ap, bp, cp)):
        coef_ref[k] = value
    nl = from_left(n, 1, low, LANES - 6)
    nr = from_right(n, 1, high, 4)
    e0, e1, e2, e3, e4 = composed(
        a0 - 2.0 * n, b0 + n, c0 + n, am - 2.0 * nl, bm + nl, cm + nl, ap - 2.0 * nr, bp + nr, cp + nr
    )
    tl1, tl2 = [from_left(t, k, low, LANES - 2) for k in (1, 2)]
    tr1, tr2 = [from_right(t, k, high, 0) for k in (1, 2)]
    heat = e0 * t + e1 * tl1 + e2 * tr1 + e3 * tl2 + e4 * tr2
    for tile in range(tiles):
        heat_ref[pl.ds(tile, levels, stride=tiles), :] = heat[:, tile * LANES : (tile + 1) * LANES]


def tracer_kernel(levels, group, tracers, q_ref, coef_ref, a_ref, b_ref, out_hbm, top_ref, new_ref, sems):
    even = lax.rem(lax.axis_index("tile"), 2) == 0
    got_a = a_ref[pl.ds(0, tracers), :]
    got_b = b_ref[pl.ds(0, tracers), :]
    low = jnp.where(even, got_b, got_a)
    high = jnp.where(even, got_a, got_b)
    copies = []
    for level in range(levels):
        q = q_ref[level]
        place = 2 * level
        e0, e1, e2, e3, e4 = [coef_ref[k, level : level + 1, :] for k in range(5)]
        new = (
            e0 * q
            + e1 * from_left(q, 1, low, place)
            + e2 * from_right(q, 1, high, place)
            + e3 * from_left(q, 2, low, place)
            + e4 * from_right(q, 2, high, place)
        )
        new_ref[level] = new
        if level == 0:
            top_ref[...] = new[:SUB]
        if level % group == group - 1:
            cut = pl.ds(level - group + 1, group)
            copies.append(pltpu.make_async_copy(new_ref.at[cut], out_hbm.at[cut], sems.at[level // group]))
            copies[-1].start()
    for copy in copies:
        copy.wait()


def surface_kernel(levels, tiles, count, m_ref, own_ref, *refs):
    got, (top_ref, mixed_ref, send_ref, whole) = refs[: count - 1], refs[count - 1 :]
    for s, ref in enumerate((own_ref,) + tuple(got)):
        whole[pl.ds(s * levels, levels), :] = wide(ref, levels, tiles)
    mixed = jnp.dot(
        m_ref[...], whole[...], precision=lax.Precision.HIGHEST, preferred_element_type=jnp.float32
    )
    mixed_ref[...] = mixed
    fields = jnp.where(
        lax.broadcasted_iota(jnp.int32, (SUB, tiles * LANES), 0) == 0,
        jnp.broadcast_to(mixed[0:1], (SUB, tiles * LANES)),
        pltpu.roll(top_ref[...], 1, 0),
    )
    for tile in range(tiles):
        send_ref[pl.ds(tile * SUB, SUB), :] = fields[:, tile * LANES : (tile + 1) * LANES]


def final_kernel(
    levels, tiles, count, sections, first_ref, mixed_ref, top_ref, index_ref, weight_ref, water_ref, *refs
):
    got, (q_ref, heat_hbm, out_ref, whole, patch, heat_ref, sems) = refs[:count], refs[count:]
    del q_ref
    width = tiles * LANES
    cells = count * width
    here = lax.axis_index("tile")
    sea = jnp.logical_and(
        lax.axis_index("comp") >= sections // 2, lax.axis_index("lev") == 0
    )
    rows = tiles * SUB
    for s in range(count):
        whole[pl.ds(pl.multiple_of(source_of(here, s, count) * rows, rows), rows), :] = got[s][...]
    first = first_ref[0]
    top = top_ref[...]
    mixed = mixed_ref[...]
    first_row = lax.broadcasted_iota(jnp.int32, (SUB, LANES), 0) == 0
    lane = lane_iota((SUB, LANES))
    for tile in range(tiles):
        cut = slice(tile * LANES, (tile + 1) * LANES)
        windows = []
        for q in range(3):
            block = lax.rem(first + tile + q - 1 + count * tiles, count * tiles)
            windows.append(whole[pl.ds(pl.multiple_of(block * SUB, SUB), SUB), :])
        total = jnp.zeros((SUB, LANES), jnp.float32)
        start = first * LANES + tile * LANES - REACH
        for k in range(index_ref.shape[0]):
            index = jnp.broadcast_to(index_ref[k : k + 1, cut], (SUB, LANES))
            weight = jnp.broadcast_to(weight_ref[k : k + 1, cut], (SUB, LANES))
            at = index - start - lane
            at = jnp.where(at < 0, at + cells, at)
            at = jnp.where(at >= cells, at - cells, at) + lane
            inner = jnp.bitwise_and(at, LANES - 1)
            outer = jnp.right_shift(at, 7)
            picks = [jnp.take_along_axis(w, inner, axis=1) for w in windows]
            picked = jnp.where(outer == 0, picks[0], jnp.where(outer == 1, picks[1], picks[2]))
            total = total + picked * weight
        own_heat = jnp.broadcast_to(mixed[0:1, cut], (SUB, LANES))
        surface = jnp.where(first_row, own_heat, pltpu.roll(top[:, cut], 1, 0))
        wet = jnp.logical_and(sea, jnp.broadcast_to(water_ref[0:1, cut], (SUB, LANES)) == 1)
        wet = jnp.logical_and(wet, lax.broadcasted_iota(jnp.int32, (SUB, LANES), 0) < NFLUX)
        renewed = jnp.where(wet, surface + 0.5 * (total - surface), surface)
        heat_ref[pl.ds(tile, levels, stride=tiles), :] = mixed[:, cut]
        heat_ref[pl.ds(tile, 1), :] = renewed[0:1]
        patch[:, cut] = jnp.where(
            lax.broadcasted_iota(jnp.int32, (SUB, LANES), 0) < NFLUX - 1,
            pltpu.roll(renewed, SUB - 1, 0),
            top[:, cut],
        )
    copies = [
        pltpu.make_async_copy(patch, out_ref.at[0, pl.ds(0, SUB), :], sems.at[0]),
        pltpu.make_async_copy(heat_ref, heat_hbm, sems.at[1]),
    ]
    for copy in copies:
        copy.start()
    for copy in copies:
        copy.wait()


def body(
    sizes,
    thermal_anomaly,
    right_face_transport_ratio,
    species_ratios,
    lateral_spreading_number,
    depth_physics_operator,
    exchange_weight_table,
    sky_point_of_entry,
    water_indicator,
):
    sections, tile_count, lev_count = sizes
    _, levels, width = thermal_anomaly.shape
    tracers = species_ratios.shape[1]
    tiles = width // LANES
    rows = levels * tiles
    f32 = jnp.float32
    shape = jax.ShapeDtypeStruct
    flat = lambda x: x.reshape(rows, LANES)
    t, u, n = flat(thermal_anomaly), flat(right_face_transport_ratio), flat(lateral_spreading_number)
    q = jnp.transpose(species_ratios, (0, 2, 1, 3)).reshape(levels, tracers, width)
    lev = lax.axis_index("lev")

    pack_rows = tracers + padded_rows(levels)
    group = 5 if levels % 5 == 0 else 1
    send_a, send_b, t_near, u_near, n_near = pl.pallas_call(
        functools.partial(pack_kernel, levels, tiles, tracers, group),
        out_shape=[shape((pack_rows, LANES), f32)] * 2 + [shape((rows, LANES), f32)] * 3,
        in_specs=[HBM] * 4,
        out_specs=[VMEM] * 5,
        scratch_shapes=[pltpu.VMEM((levels, tracers, LANES), f32)] * 2
        + [pltpu.SemaphoreType.DMA((3, max(3, levels // group)))],
        compiler_params=PARAMS,
        name="pack",
    )(*(pltpu.with_memory_space_constraint(x, pltpu.HBM) for x in (t, u, n, q)))
    swap_a = [(i, i ^ 1) for i in range(tile_count)]
    swap_b = [(i, (i + 1) % tile_count if i % 2 else (i - 1) % tile_count) for i in range(tile_count)]
    got_a = lax.ppermute(send_a, "tile", swap_a)
    got_b = lax.ppermute(send_b, "tile", swap_b)

    heat, coef = pl.pallas_call(
        functools.partial(heat_kernel, levels, tiles, tracers, sections),
        out_shape=[shape((rows, LANES), f32), shape((5, levels, width), f32)],
        in_specs=[VMEM] * 5,
        out_specs=[VMEM, VMEM],
        compiler_params=PARAMS,
        name="heat",
    )(t_near, u_near, n_near, got_a, got_b)

    others = [
        lax.ppermute(heat, "lev", [(i, peer(i, s, lev_count)) for i in range(lev_count)])
        for s in range(1, lev_count)
    ]

    moved, top = pl.pallas_call(
        functools.partial(tracer_kernel, levels, group, tracers),
        out_shape=[shape((levels, tracers, width), f32), shape((SUB, width), f32)],
        in_specs=[VMEM] * 4,
        out_specs=[HBM, VMEM],
        scratch_shapes=[
            pltpu.VMEM((levels, tracers, width), f32),
            pltpu.SemaphoreType.DMA((levels // group,)),
        ],
        cost_estimate=pl.CostEstimate(
            flops=9 * levels * tracers * width, bytes_accessed=8 * levels * tracers * width, transcendentals=0
        ),
        compiler_params=PARAMS,
        name="tracers",
    )(q, coef, got_a, got_b)

    mine = lax.dynamic_slice_in_dim(depth_physics_operator[0], lev * levels, levels, 0)
    columns = [
        lax.dynamic_slice_in_dim(mine, source_of(lev, s, lev_count) * levels, levels, 1)
        for s in range(lev_count)
    ]
    matrix = jnp.concatenate(columns, axis=1)
    mixed, surface = pl.pallas_call(
        functools.partial(surface_kernel, levels, tiles, lev_count),
        out_shape=[shape((levels, width), f32), shape((tiles * SUB, LANES), f32)],
        in_specs=[VMEM] * (lev_count + 2),
        out_specs=[VMEM, VMEM],
        scratch_shapes=[pltpu.VMEM((levels * lev_count, width), f32)],
        compiler_params=PARAMS,
        name="surface",
    )(matrix, heat, *others, top)

    half = sections // 2
    place = lambda c, i, l: (c * tile_count + i) * lev_count + l
    got = [
        lax.ppermute(
            surface,
            ("comp", "tile", "lev"),
            [
                (place(c, i, l), place((c + half) % sections, peer(i, s, tile_count), l))
                for c in range(sections)
                for i in range(tile_count)
                for l in range(lev_count)
            ],
        )
        for s in range(tile_count)
    ]

    index = sky_point_of_entry.T
    cells = tile_count * width
    first = ((index[0, 0:1] + REACH) % cells) // width * tiles
    heat_out, q_out = pl.pallas_call(
        functools.partial(final_kernel, levels, tiles, tile_count, sections),
        out_shape=[shape((rows, LANES), f32), shape((levels, tracers, width), f32)],
        in_specs=[SMEM] + [VMEM] * (5 + tile_count) + [HBM],
        out_specs=[HBM, HBM],
        scratch_shapes=[
            pltpu.VMEM((tile_count * tiles * SUB, LANES), f32),
            pltpu.VMEM((SUB, width), f32),
            pltpu.VMEM((rows, LANES), f32),
            pltpu.SemaphoreType.DMA((2,)),
        ],
        input_output_aliases={6 + tile_count: 1},
        compiler_params=PARAMS,
        name="remap",
    )(
        first, mixed, top, index, exchange_weight_table.T, water_indicator.reshape(1, width), *got, moved
    )
    thermal_anomaly_ending = heat_out.reshape(1, levels, width)
    species_ratios_ending = jnp.transpose(q_out.reshape(1, levels, tracers, width), (0, 2, 1, 3))
    return thermal_anomaly_ending, species_ratios_ending


def solution(mesh):
    in_specs = (
        P("comp", "lev", "tile"),
        P("comp", "lev", "tile"),
        P("comp", None, "lev", "tile"),
        P("comp", "lev", "tile"),
        P("comp", None, None),
        P("tile", None),
        P("tile", None),
        P("tile"),
    )
    out_specs = (P("comp", "lev", "tile"), P("comp", None, "lev", "tile"))
    sizes = (mesh.shape["comp"], mesh.shape["tile"], mesh.shape["lev"])
    return jax.shard_map(
        functools.partial(body, sizes), mesh=mesh, in_specs=in_specs, out_specs=out_specs, check_vma=False
    )
```

```python
import functools

import jax
import jax.numpy as jnp
from jax import lax
from jax.experimental import pallas as pl
from jax.experimental.pallas import tpu as pltpu
from jax.sharding import PartitionSpec as P


NFLUX = 4
LANES = 128
SUB = 8
REACH = 128
T_AT, U_AT, N_AT = LANES - 6, LANES - 4, LANES - 2

VMEM = pl.BlockSpec(memory_space=pltpu.VMEM)
HBM = pl.BlockSpec(memory_space=pltpu.HBM)
PARAMS = pltpu.CompilerParams(vmem_limit_bytes=8 * 2**20)


def peer(i, s, n):
    return i ^ s if n & (n - 1) == 0 else (i + s) % n


def source_of(me, s, n):
    return me ^ s if n & (n - 1) == 0 else lax.rem(me - s + n, n)


def lane_iota(shape):
    return lax.broadcasted_iota(jnp.int32, shape, len(shape) - 1)


def wide(ref, levels, tiles):
    return jnp.concatenate([ref[pl.ds(t, levels, stride=tiles), :] for t in range(tiles)], axis=1)


def from_left(x, k, halo, place):
    moved = pltpu.roll(x, k, 1)
    edge = pltpu.roll(halo, (k - place - 2) % LANES, 1)
    head = jnp.where(lane_iota(edge.shape) < k, edge, moved[:, :LANES])
    return jnp.concatenate([head, moved[:, LANES:]], axis=1)


def from_right(x, k, halo, place):
    width = x.shape[1]
    moved = pltpu.roll(x, width - k, 1)
    edge = pltpu.roll(halo, (-k - place) % LANES, 1)
    tail = jnp.where(lane_iota(edge.shape) >= LANES - k, edge, moved[:, width - LANES :])
    return jnp.concatenate([moved[:, : width - LANES], tail], axis=1)


def pack_kernel(
    levels, tiles, tracers, group, t_hbm, u_hbm, n_hbm, q_hbm, a_ref, b_ref, t_ref, u_ref, n_ref, left, right, sems
):
    width = tiles * LANES
    flats = [
        pltpu.make_async_copy(source, target, sems.at[0, i])
        for i, (source, target) in enumerate(((t_hbm, t_ref), (u_hbm, u_ref), (n_hbm, n_ref)))
    ]
    chunks = []
    for g in range(levels // group):
        cut = pl.ds(g * group, group)
        chunks.append(
            [
                pltpu.make_async_copy(q_hbm.at[cut, :, pl.ds(0, LANES)], left.at[cut], sems.at[1, g]),
                pltpu.make_async_copy(q_hbm.at[cut, :, pl.ds(width - LANES, LANES)], right.at[cut], sems.at[2, g]),
            ]
        )
    for copy in flats:
        copy.start()
    for chunk in chunks:
        for copy in chunk:
            copy.start()
    even = lax.rem(lax.axis_index("tile"), 2) == 0
    lane = lane_iota((levels, LANES))

    def small(row, edge):
        t, u, n = [
            pltpu.roll(r[pl.ds(row, levels, stride=tiles), :], (at - edge) % LANES, 1)
            for r, at in ((t_ref, T_AT), (u_ref, U_AT), (n_ref, N_AT))
        ]
        return jnp.where(lane < U_AT, t, jnp.where(lane < N_AT, u, n))

    for copy in flats:
        copy.wait()
    fill = jnp.zeros((tracers - levels, LANES), jnp.float32)
    packed_left = jnp.concatenate([small(0, 0), fill], axis=0)
    packed_right = jnp.concatenate([small(tiles - 1, LANES - 2), fill], axis=0)
    pair = lane_iota((tracers, LANES)) // 2
    for g, chunk in enumerate(chunks):
        for copy in chunk:
            copy.wait()
        for level in range(g * group, (g + 1) * group):
            here = pair == level
            packed_left = jnp.where(here, pltpu.roll(left[level], 2 * level, 1), packed_left)
            packed_right = jnp.where(here, pltpu.roll(right[level], (2 * level + 2) % LANES, 1), packed_right)
    a_ref[...] = jnp.where(even, packed_right, packed_left)
    b_ref[...] = jnp.where(even, packed_left, packed_right)


def heat_kernel(levels, tiles, sections, t_ref, u_ref, n_ref, a_ref, b_ref, heat_ref, coef_ref):
    even = lax.rem(lax.axis_index("tile"), 2) == 0
    ocean = lax.axis_index("comp") >= sections // 2
    t, u, n = [wide(r, levels, tiles) for r in (t_ref, u_ref, n_ref)]
    got_a = a_ref[pl.ds(0, levels), :]
    got_b = b_ref[pl.ds(0, levels), :]
    low = jnp.where(even, got_b, got_a)
    high = jnp.where(even, got_a, got_b)
    ul1, ul2 = [from_left(u, k, low, U_AT) for k in (1, 2)]
    ur1 = from_right(u, 1, high, U_AT)
    plus = lambda v: jnp.maximum(v, 0.0)
    minus = lambda v: jnp.minimum(v, 0.0)
    a0, b0, c0 = 1.0 - plus(u) + minus(ul1), plus(ul1), -minus(u)
    am, bm, cm = 1.0 - plus(ul1) + minus(ul2), plus(ul2), -minus(ul1)
    ap, bp, cp = 1.0 - plus(ur1) + minus(u), plus(u), -minus(ur1)

    def composed(a0, b0, c0, am, bm, cm, ap, bp, cp):
        return (
            jnp.where(ocean, a0, a0 * a0 + b0 * cm + c0 * bp),
            jnp.where(ocean, b0, b0 * (a0 + am)),
            jnp.where(ocean, c0, c0 * (a0 + ap)),
            jnp.where(ocean, 0.0, b0 * bm),
            jnp.where(ocean, 0.0, c0 * cp),
        )

    for k, value in enumerate(composed(a0, b0, c0, am, bm, cm, ap, bp, cp)):
        coef_ref[k] = value
    nl = from_left(n, 1, low, N_AT)
    nr = from_right(n, 1, high, N_AT)
    e0, e1, e2, e3, e4 = composed(
        a0 - 2.0 * n, b0 + n, c0 + n, am - 2.0 * nl, bm + nl, cm + nl, ap - 2.0 * nr, bp + nr, cp + nr
    )
    tl1, tl2 = [from_left(t, k, low, T_AT) for k in (1, 2)]
    tr1, tr2 = [from_right(t, k, high, T_AT) for k in (1, 2)]
    heat = e0 * t + e1 * tl1 + e2 * tr1 + e3 * tl2 + e4 * tr2
    for tile in range(tiles):
        heat_ref[pl.ds(tile, levels, stride=tiles), :] = heat[:, tile * LANES : (tile + 1) * LANES]


def plan(tiles, count, index_ref, first_ref, inner_ref, outer_ref):
    width = tiles * LANES
    cells = count * width
    index = index_ref[...]
    lane = lane_iota(index.shape)
    corner = jnp.max(jnp.where(lane_iota((1, LANES)) == 0, index[0:1, :LANES], 0))
    block = lax.rem(corner + REACH, cells) // width
    first_ref[...] = jnp.full(first_ref.shape, block * tiles, jnp.int32)
    at = index - (block * width - REACH) - lane
    at = jnp.where(at < 0, at + cells, at)
    at = jnp.where(at >= cells, at - cells, at) + jnp.bitwise_and(lane, LANES - 1)
    inner_ref[...] = jnp.bitwise_and(at, LANES - 1)
    outer_ref[...] = jnp.right_shift(at, 7)


def advance(levels, group, q_ref, coef_ref, a_ref, b_ref, out_hbm, new_ref, sems, top_ref):
    even = lax.rem(lax.axis_index("tile"), 2) == 0
    low = jnp.where(even, b_ref[...], a_ref[...])
    high = jnp.where(even, a_ref[...], b_ref[...])
    copies = []
    for level in range(levels):
        q = q_ref[level]
        place = 2 * level
        e0, e1, e2, e3, e4 = [coef_ref[k, level : level + 1, :] for k in range(5)]
        new = (
            e0 * q
            + e1 * from_left(q, 1, low, place)
            + e2 * from_right(q, 1, high, place)
            + e3 * from_left(q, 2, low, place)
            + e4 * from_right(q, 2, high, place)
        )
        new_ref[level] = new
        if level == 0:
            top_ref[...] = new[:SUB]
        if level % group == group - 1:
            cut = pl.ds(level - group + 1, group)
            copies.append(pltpu.make_async_copy(new_ref.at[cut], out_hbm.at[cut], sems.at[level // group]))
            copies[-1].start()
    for copy in copies:
        copy.wait()


def tracer_kernel(
    levels, group, tiles, count,
    q_ref, coef_ref, a_ref, b_ref, index_ref,
    out_hbm, top_ref, first_ref, inner_ref, outer_ref, new_ref, sems,
):
    plan(tiles, count, index_ref, first_ref, inner_ref, outer_ref)
    advance(levels, group, q_ref, coef_ref, a_ref, b_ref, out_hbm, new_ref, sems, top_ref)


def surface_kernel(levels, tiles, count, m_ref, own_ref, *refs):
    got, (top_ref, mixed_ref, send_ref, whole) = refs[: count - 1], refs[count - 1 :]
    for s, ref in enumerate((own_ref,) + tuple(got)):
        whole[pl.ds(s * levels, levels), :] = wide(ref, levels, tiles)
    mixed = jnp.dot(
        m_ref[...], whole[...], precision=lax.Precision.HIGHEST, preferred_element_type=jnp.float32
    )
    mixed_ref[...] = mixed
    fields = jnp.where(
        lax.broadcasted_iota(jnp.int32, (SUB, tiles * LANES), 0) == 0,
        jnp.broadcast_to(mixed[0:1], (SUB, tiles * LANES)),
        pltpu.roll(top_ref[...], 1, 0),
    )
    for tile in range(tiles):
        send_ref[pl.ds(tile * NFLUX, NFLUX), :] = fields[:NFLUX, tile * LANES : (tile + 1) * LANES]


def final_kernel(
    levels, tiles, count, sections, first_ref, inner_ref, outer_ref, mixed_ref, top_ref, weight_ref, water_ref, *refs
):
    got, (q_ref, heat_hbm, out_ref, whole, patch, heat_ref, sems) = refs[:count], refs[count:]
    del q_ref
    here = lax.axis_index("tile")
    sea = jnp.logical_and(
        lax.axis_index("comp") >= sections // 2, lax.axis_index("lev") == 0
    )
    for s in range(count):
        base = (here ^ s) * tiles * SUB
        for tile in range(tiles):
            whole[pl.ds(pl.multiple_of(base + tile * SUB, SUB), NFLUX), :] = got[s][pl.ds(tile * NFLUX, NFLUX), :]
    first = jnp.max(first_ref[...])
    top = top_ref[...]
    mixed = mixed_ref[...]
    first_row = lax.broadcasted_iota(jnp.int32, (SUB, LANES), 0) == 0
    lane = lane_iota((SUB, LANES))
    for tile in range(tiles):
        cut = slice(tile * LANES, (tile + 1) * LANES)
        windows = []
        for q in range(3):
            block = lax.rem(first + tile + q - 1 + count * tiles, count * tiles)
            windows.append(whole[pl.ds(pl.multiple_of(block * SUB, SUB), SUB), :])
        total = jnp.zeros((SUB, LANES), jnp.float32)
        for k in range(weight_ref.shape[0]):
            weight = jnp.broadcast_to(weight_ref[k : k + 1, cut], (SUB, LANES))
            inner = jnp.broadcast_to(inner_ref[k : k + 1, cut], (SUB, LANES))
            outer = jnp.broadcast_to(outer_ref[k : k + 1, cut], (SUB, LANES))
            picks = [jnp.take_along_axis(w, inner, axis=1) for w in windows]
            picked = jnp.where(outer == 0, picks[0], jnp.where(outer == 1, picks[1], picks[2]))
            total = total + picked * weight
        own_heat = jnp.broadcast_to(mixed[0:1, cut], (SUB, LANES))
        surface = jnp.where(first_row, own_heat, pltpu.roll(top[:, cut], 1, 0))
        wet = jnp.logical_and(sea, jnp.broadcast_to(water_ref[0:1, cut], (SUB, LANES)) == 1)
        wet = jnp.logical_and(wet, lax.broadcasted_iota(jnp.int32, (SUB, LANES), 0) < NFLUX)
        renewed = jnp.where(wet, surface + 0.5 * (total - surface), surface)
        heat_ref[pl.ds(tile, levels, stride=tiles), :] = mixed[:, cut]
        heat_ref[pl.ds(tile, 1), :] = renewed[0:1]
        patch[:, cut] = jnp.where(
            lax.broadcasted_iota(jnp.int32, (SUB, LANES), 0) < NFLUX - 1,
            pltpu.roll(renewed, SUB - 1, 0),
            top[:, cut],
        )
    copies = [
        pltpu.make_async_copy(patch, out_ref.at[0, pl.ds(0, SUB), :], sems.at[0]),
        pltpu.make_async_copy(heat_ref, heat_hbm, sems.at[1]),
    ]
    for copy in copies:
        copy.start()
    for copy in copies:
        copy.wait()


def interval(
    sizes,
    thermal_anomaly,
    right_face_transport_ratio,
    species_ratios,
    lateral_spreading_number,
    depth_physics_operator,
    exchange_weight_table,
    sky_point_of_entry,
    water_indicator,
):
    sections, tile_count, lev_count = sizes
    _, levels, width = thermal_anomaly.shape
    tracers = species_ratios.shape[1]
    tiles = width // LANES
    rows = levels * tiles
    f32 = jnp.float32
    shape = jax.ShapeDtypeStruct
    flat = lambda x: x.reshape(rows, LANES)
    t, u, n = flat(thermal_anomaly), flat(right_face_transport_ratio), flat(lateral_spreading_number)
    q = jnp.transpose(species_ratios, (0, 2, 1, 3)).reshape(levels, tracers, width)
    lev = lax.axis_index("lev")

    pack_rows = tracers
    group = 5 if levels % 5 == 0 else 1
    send_a, send_b, t_near, u_near, n_near = pl.pallas_call(
        functools.partial(pack_kernel, levels, tiles, tracers, group),
        out_shape=[shape((pack_rows, LANES), f32)] * 2 + [shape((rows, LANES), f32)] * 3,
        in_specs=[HBM] * 4,
        out_specs=[VMEM] * 5,
        scratch_shapes=[pltpu.VMEM((levels, tracers, LANES), f32)] * 2
        + [pltpu.SemaphoreType.DMA((3, max(3, levels // group)))],
        compiler_params=PARAMS,
        name="pack",
    )(*(pltpu.with_memory_space_constraint(x, pltpu.HBM) for x in (t, u, n, q)))
    swap_a = [(i, i ^ 1) for i in range(tile_count)]
    swap_b = [(i, (i + 1) % tile_count if i % 2 else (i - 1) % tile_count) for i in range(tile_count)]
    got_a = lax.ppermute(send_a, "tile", swap_a)
    got_b = lax.ppermute(send_b, "tile", swap_b)

    heat, coef = pl.pallas_call(
        functools.partial(heat_kernel, levels, tiles, sections),
        out_shape=[shape((rows, LANES), f32), shape((5, levels, width), f32)],
        in_specs=[VMEM] * 5,
        out_specs=[VMEM, VMEM],
        compiler_params=PARAMS,
        name="heat",
    )(t_near, u_near, n_near, got_a, got_b)

    others = [
        lax.ppermute(heat, "lev", [(i, peer(i, s, lev_count)) for i in range(lev_count)])
        for s in range(1, lev_count)
    ]

    index = sky_point_of_entry.T
    estimate = pl.CostEstimate(
        flops=9 * levels * tracers * width, bytes_accessed=8 * levels * tracers * width, transcendentals=0
    )
    buffers = [pltpu.VMEM((levels, tracers, width), f32), pltpu.SemaphoreType.DMA((levels,))]
    moved, top, first, inner, outer = pl.pallas_call(
        functools.partial(tracer_kernel, levels, group, tiles, tile_count),
        out_shape=[
            shape((levels, tracers, width), f32),
            shape((SUB, width), f32),
            shape((1, LANES), jnp.int32),
            shape(index.shape, jnp.int32),
            shape(index.shape, jnp.int32),
        ],
        in_specs=[VMEM] * 5,
        out_specs=[HBM] + [VMEM] * 4,
        scratch_shapes=buffers,
        cost_estimate=estimate,
        compiler_params=PARAMS,
        name="tracers",
    )(q, coef, got_a, got_b, index)

    mine = lax.dynamic_slice_in_dim(depth_physics_operator[0], lev * levels, levels, 0)
    columns = [
        lax.dynamic_slice_in_dim(mine, source_of(lev, s, lev_count) * levels, levels, 1)
        for s in range(lev_count)
    ]
    matrix = jnp.concatenate(columns, axis=1)
    mixed, surface = pl.pallas_call(
        functools.partial(surface_kernel, levels, tiles, lev_count),
        out_shape=[shape((levels, width), f32), shape((tiles * NFLUX, LANES), f32)],
        in_specs=[VMEM] * (lev_count + 2),
        out_specs=[VMEM, VMEM],
        scratch_shapes=[pltpu.VMEM((levels * lev_count, width), f32)],
        compiler_params=PARAMS,
        name="surface",
    )(matrix, heat, *others, top)

    half = sections // 2
    place = lambda c, i, l: (c * tile_count + i) * lev_count + l

    def across(s):
        pairs = [
            (place(c, i, l), place((c + half) % sections, i ^ s, l))
            for c in range(sections)
            for i in range(tile_count)
            for l in range(lev_count)
        ]
        return lax.ppermute(surface, ("comp", "tile", "lev"), pairs)

    got = [None] * tile_count
    for s in range(1, tile_count, 2):
        got[s] = across(s)
    for s in range(1, tile_count, 2):
        got[s ^ 1] = lax.ppermute(got[s], "tile", swap_a)

    heat_out, q_out = pl.pallas_call(
        functools.partial(final_kernel, levels, tiles, tile_count, sections),
        out_shape=[shape((rows, LANES), f32), shape((levels, tracers, width), f32)],
        in_specs=[VMEM] * (7 + tile_count) + [HBM],
        out_specs=[HBM, HBM],
        scratch_shapes=[
            pltpu.VMEM((tile_count * tiles * SUB, LANES), f32),
            pltpu.VMEM((SUB, width), f32),
            pltpu.VMEM((rows, LANES), f32),
            pltpu.SemaphoreType.DMA((2,)),
        ],
        input_output_aliases={7 + tile_count: 1},
        compiler_params=PARAMS,
        name="remap",
    )(
        first, inner, outer, mixed, top, exchange_weight_table.T, water_indicator.reshape(1, width), *got, moved
    )
    thermal_anomaly_ending = heat_out.reshape(1, levels, width)
    species_ratios_ending = jnp.transpose(q_out.reshape(1, levels, tracers, width), (0, 2, 1, 3))
    return thermal_anomaly_ending, species_ratios_ending


def solution(mesh):
    in_specs = (
        P("comp", "lev", "tile"),
        P("comp", "lev", "tile"),
        P("comp", None, "lev", "tile"),
        P("comp", "lev", "tile"),
        P("comp", None, None),
        P("tile", None),
        P("tile", None),
        P("tile"),
    )
    out_specs = (P("comp", "lev", "tile"), P("comp", None, "lev", "tile"))
    sizes = (mesh.shape["comp"], mesh.shape["tile"], mesh.shape["lev"])
    return jax.shard_map(
        functools.partial(interval, sizes), mesh=mesh, in_specs=in_specs, out_specs=out_specs, check_vma=False
    )
```

```python
import functools

import jax
import jax.numpy as jnp
from jax import lax
from jax.experimental import pallas as pl
from jax.experimental.pallas import tpu as pltpu
from jax.sharding import PartitionSpec as P


NFLUX = 4
LANES = 128
SUB = 8
REACH = 128
T_AT, U_AT, N_AT = LANES - 6, LANES - 4, LANES - 2

VMEM = pl.BlockSpec(memory_space=pltpu.VMEM)
HBM = pl.BlockSpec(memory_space=pltpu.HBM)
PARAMS = pltpu.CompilerParams(vmem_limit_bytes=8 * 2**20)


def peer(i, s, n):
    return i ^ s if n & (n - 1) == 0 else (i + s) % n


def source_of(me, s, n):
    return me ^ s if n & (n - 1) == 0 else lax.rem(me - s + n, n)


def lane_iota(shape):
    return lax.broadcasted_iota(jnp.int32, shape, len(shape) - 1)


def wide(ref, levels, tiles):
    return jnp.concatenate([ref[pl.ds(t, levels, stride=tiles), :] for t in range(tiles)], axis=1)


def from_left(x, k, halo, place):
    moved = pltpu.roll(x, k, 1)
    edge = pltpu.roll(halo, (k - place - 2) % LANES, 1)
    head = jnp.where(lane_iota(edge.shape) < k, edge, moved[:, :LANES])
    return jnp.concatenate([head, moved[:, LANES:]], axis=1)


def from_right(x, k, halo, place):
    width = x.shape[1]
    moved = pltpu.roll(x, width - k, 1)
    edge = pltpu.roll(halo, (-k - place) % LANES, 1)
    tail = jnp.where(lane_iota(edge.shape) >= LANES - k, edge, moved[:, width - LANES :])
    return jnp.concatenate([moved[:, : width - LANES], tail], axis=1)


def edge_kernel(
    levels, tiles, t_hbm, u_hbm, n_hbm, q_hbm, a_ref, b_ref, t_ref, u_ref, n_ref, top_ref, sems
):
    copies = [
        pltpu.make_async_copy(source, target, sems.at[i])
        for i, (source, target) in enumerate(
            ((t_hbm, t_ref), (u_hbm, u_ref), (n_hbm, n_ref), (q_hbm.at[0, pl.ds(0, SUB), :], top_ref))
        )
    ]
    for copy in copies:
        copy.start()
    even = lax.rem(lax.axis_index("tile"), 2) == 0
    lane = lane_iota((levels, LANES))

    def small(tile, edge):
        t, u, n = [
            pltpu.roll(r[pl.ds(tile, levels, stride=tiles), :], (at - edge) % LANES, 1)
            for r, at in ((t_ref, T_AT), (u_ref, U_AT), (n_ref, N_AT))
        ]
        top = pltpu.roll(top_ref[:, tile * LANES : (tile + 1) * LANES], -edge % LANES, 1)
        top = jnp.concatenate([top, jnp.zeros((levels - SUB, LANES), jnp.float32)], axis=0)
        return jnp.where(lane < 2, top, jnp.where(lane < U_AT, t, jnp.where(lane < N_AT, u, n)))

    for copy in copies:
        copy.wait()
    left = small(0, 0)
    right = small(tiles - 1, LANES - 2)
    a_ref[...] = jnp.where(even, right, left)
    b_ref[...] = jnp.where(even, left, right)


def pack_kernel(levels, tiles, group, q_hbm, a_ref, b_ref, left, right, sems):
    width = tiles * LANES
    chunks = []
    for g in range(levels // group):
        cut = pl.ds(g * group, group)
        chunks.append(
            [
                pltpu.make_async_copy(q_hbm.at[cut, :, pl.ds(0, LANES)], left.at[cut], sems.at[0, g]),
                pltpu.make_async_copy(q_hbm.at[cut, :, pl.ds(width - LANES, LANES)], right.at[cut], sems.at[1, g]),
            ]
        )
        for copy in chunks[-1]:
            copy.start()
    even = lax.rem(lax.axis_index("tile"), 2) == 0
    tracers = a_ref.shape[0]
    pair = lane_iota((tracers, LANES)) // 2
    packed_left = packed_right = jnp.zeros((tracers, LANES), jnp.float32)
    for g, chunk in enumerate(chunks):
        for copy in chunk:
            copy.wait()
        for level in range(g * group, (g + 1) * group):
            here = pair == level
            packed_left = jnp.where(here, pltpu.roll(left[level], 2 * level, 1), packed_left)
            packed_right = jnp.where(here, pltpu.roll(right[level], (2 * level + 2) % LANES, 1), packed_right)
    a_ref[...] = jnp.where(even, packed_right, packed_left)
    b_ref[...] = jnp.where(even, packed_left, packed_right)


def heat_kernel(levels, tiles, sections, t_ref, u_ref, n_ref, near_ref, a_ref, b_ref, heat_ref, coef_ref, top_ref):
    even = lax.rem(lax.axis_index("tile"), 2) == 0
    ocean = lax.axis_index("comp") >= sections // 2
    t, u, n = [wide(r, levels, tiles) for r in (t_ref, u_ref, n_ref)]
    low = jnp.where(even, b_ref[...], a_ref[...])
    high = jnp.where(even, a_ref[...], b_ref[...])
    ul1, ul2 = [from_left(u, k, low, U_AT) for k in (1, 2)]
    ur1 = from_right(u, 1, high, U_AT)
    plus = lambda v: jnp.maximum(v, 0.0)
    minus = lambda v: jnp.minimum(v, 0.0)
    a0, b0, c0 = 1.0 - plus(u) + minus(ul1), plus(ul1), -minus(u)
    am, bm, cm = 1.0 - plus(ul1) + minus(ul2), plus(ul2), -minus(ul1)
    ap, bp, cp = 1.0 - plus(ur1) + minus(u), plus(u), -minus(ur1)

    def composed(a0, b0, c0, am, bm, cm, ap, bp, cp):
        return (
            jnp.where(ocean, a0, a0 * a0 + b0 * cm + c0 * bp),
            jnp.where(ocean, b0, b0 * (a0 + am)),
            jnp.where(ocean, c0, c0 * (a0 + ap)),
            jnp.where(ocean, 0.0, b0 * bm),
            jnp.where(ocean, 0.0, c0 * cp),
        )

    shared = composed(a0, b0, c0, am, bm, cm, ap, bp, cp)
    for k, value in enumerate(shared):
        coef_ref[k] = value
    q = near_ref[...]
    f0, f1, f2, f3, f4 = [value[0:1] for value in shared]
    top_low, top_high = low[:SUB], high[:SUB]
    top_ref[...] = (
        f0 * q
        + f1 * from_left(q, 1, top_low, 0)
        + f2 * from_right(q, 1, top_high, 0)
        + f3 * from_left(q, 2, top_low, 0)
        + f4 * from_right(q, 2, top_high, 0)
    )
    nl = from_left(n, 1, low, N_AT)
    nr = from_right(n, 1, high, N_AT)
    e0, e1, e2, e3, e4 = composed(
        a0 - 2.0 * n, b0 + n, c0 + n, am - 2.0 * nl, bm + nl, cm + nl, ap - 2.0 * nr, bp + nr, cp + nr
    )
    tl1, tl2 = [from_left(t, k, low, T_AT) for k in (1, 2)]
    tr1, tr2 = [from_right(t, k, high, T_AT) for k in (1, 2)]
    heat = e0 * t + e1 * tl1 + e2 * tr1 + e3 * tl2 + e4 * tr2
    for tile in range(tiles):
        heat_ref[pl.ds(tile, levels, stride=tiles), :] = heat[:, tile * LANES : (tile + 1) * LANES]


def plan(tiles, count, index_ref, first_ref, inner_ref, outer_ref):
    width = tiles * LANES
    cells = count * width
    index = index_ref[...]
    lane = lane_iota(index.shape)
    corner = jnp.max(jnp.where(lane_iota((1, LANES)) == 0, index[0:1, :LANES], 0))
    block = lax.rem(corner + REACH, cells) // width
    first_ref[...] = jnp.full(first_ref.shape, block * tiles, jnp.int32)
    at = index - (block * width - REACH) - lane
    at = jnp.where(at < 0, at + cells, at)
    at = jnp.where(at >= cells, at - cells, at) + jnp.bitwise_and(lane, LANES - 1)
    inner_ref[...] = jnp.bitwise_and(at, LANES - 1)
    outer_ref[...] = jnp.right_shift(at, 7)


def inner_kernel(
    levels, tiles, count, q_ref, coef_ref, index_ref, new_ref, first_ref, inner_ref, outer_ref
):
    plan(tiles, count, index_ref, first_ref, inner_ref, outer_ref)
    none = jnp.zeros((q_ref.shape[1], LANES), jnp.float32)
    for level in range(levels):
        q = q_ref[level]
        e0, e1, e2, e3, e4 = [coef_ref[k, level : level + 1, :] for k in range(5)]
        new_ref[level] = (
            e0 * q
            + e1 * from_left(q, 1, none, 0)
            + e2 * from_right(q, 1, none, 0)
            + e3 * from_left(q, 2, none, 0)
            + e4 * from_right(q, 2, none, 0)
        )


def outer_kernel(levels, tiles, group, part_ref, coef_ref, a_ref, b_ref, after_ref, out_hbm, new_ref, sems):
    del after_ref
    even = lax.rem(lax.axis_index("tile"), 2) == 0
    low = jnp.where(even, b_ref[...], a_ref[...])
    high = jnp.where(even, a_ref[...], b_ref[...])
    lane = lane_iota(low.shape)
    head, last = slice(0, LANES), slice((tiles - 1) * LANES, tiles * LANES)
    copies = []
    for level in range(levels):
        new_ref[level] = part_ref[level]
        added = jnp.zeros(low.shape, jnp.float32)
        for k, e in ((1, 1), (2, 3)):
            halo = pltpu.roll(low, (k - 2 * level - 2) % LANES, 1)
            added = added + coef_ref[e, level : level + 1, head] * jnp.where(lane < k, halo, 0.0)
        new_ref[level, :, head] = part_ref[level, :, head] + added
        added = jnp.zeros(low.shape, jnp.float32)
        for k, e in ((1, 2), (2, 4)):
            halo = pltpu.roll(high, (-k - 2 * level) % LANES, 1)
            added = added + coef_ref[e, level : level + 1, last] * jnp.where(lane >= LANES - k, halo, 0.0)
        new_ref[level, :, last] = (new_ref if tiles == 1 else part_ref)[level, :, last] + added
        if level % group == group - 1:
            cut = pl.ds(level - group + 1, group)
            copies.append(pltpu.make_async_copy(new_ref.at[cut], out_hbm.at[cut], sems.at[level // group]))
            copies[-1].start()
    for copy in copies:
        copy.wait()


def surface_kernel(levels, tiles, count, m_ref, own_ref, *refs):
    got, (top_ref, mixed_ref, send_ref, whole) = refs[: count - 1], refs[count - 1 :]
    for s, ref in enumerate((own_ref,) + tuple(got)):
        whole[pl.ds(s * levels, levels), :] = wide(ref, levels, tiles)
    mixed = jnp.dot(
        m_ref[...], whole[...], precision=lax.Precision.HIGHEST, preferred_element_type=jnp.float32
    )
    mixed_ref[...] = mixed
    fields = jnp.where(
        lax.broadcasted_iota(jnp.int32, (SUB, tiles * LANES), 0) == 0,
        jnp.broadcast_to(mixed[0:1], (SUB, tiles * LANES)),
        pltpu.roll(top_ref[...], 1, 0),
    )
    for tile in range(tiles):
        send_ref[pl.ds(tile * NFLUX, NFLUX), :] = fields[:NFLUX, tile * LANES : (tile + 1) * LANES]


def final_kernel(
    levels, tiles, count, sections, first_ref, inner_ref, outer_ref, mixed_ref, top_ref, weight_ref, water_ref, *refs
):
    got, (q_ref, heat_hbm, out_ref, whole, patch, heat_ref, sems) = refs[:count], refs[count:]
    del q_ref
    here = lax.axis_index("tile")
    sea = jnp.logical_and(
        lax.axis_index("comp") >= sections // 2, lax.axis_index("lev") == 0
    )
    for s in range(count):
        base = (here ^ s) * tiles * SUB
        for tile in range(tiles):
            whole[pl.ds(pl.multiple_of(base + tile * SUB, SUB), NFLUX), :] = got[s][pl.ds(tile * NFLUX, NFLUX), :]
    first = jnp.max(first_ref[...])
    top = top_ref[...]
    mixed = mixed_ref[...]
    first_row = lax.broadcasted_iota(jnp.int32, (SUB, LANES), 0) == 0
    lane = lane_iota((SUB, LANES))
    for tile in range(tiles):
        cut = slice(tile * LANES, (tile + 1) * LANES)
        windows = []
        for q in range(3):
            block = lax.rem(first + tile + q - 1 + count * tiles, count * tiles)
            windows.append(whole[pl.ds(pl.multiple_of(block * SUB, SUB), SUB), :])
        total = jnp.zeros((SUB, LANES), jnp.float32)
        for k in range(weight_ref.shape[0]):
            weight = jnp.broadcast_to(weight_ref[k : k + 1, cut], (SUB, LANES))
            inner = jnp.broadcast_to(inner_ref[k : k + 1, cut], (SUB, LANES))
            outer = jnp.broadcast_to(outer_ref[k : k + 1, cut], (SUB, LANES))
            picks = [jnp.take_along_axis(w, inner, axis=1) for w in windows]
            picked = jnp.where(outer == 0, picks[0], jnp.where(outer == 1, picks[1], picks[2]))
            total = total + picked * weight
        own_heat = jnp.broadcast_to(mixed[0:1, cut], (SUB, LANES))
        surface = jnp.where(first_row, own_heat, pltpu.roll(top[:, cut], 1, 0))
        wet = jnp.logical_and(sea, jnp.broadcast_to(water_ref[0:1, cut], (SUB, LANES)) == 1)
        wet = jnp.logical_and(wet, lax.broadcasted_iota(jnp.int32, (SUB, LANES), 0) < NFLUX)
        renewed = jnp.where(wet, surface + 0.5 * (total - surface), surface)
        heat_ref[pl.ds(tile, levels, stride=tiles), :] = mixed[:, cut]
        heat_ref[pl.ds(tile, 1), :] = renewed[0:1]
        patch[:, cut] = jnp.where(
            lax.broadcasted_iota(jnp.int32, (SUB, LANES), 0) < NFLUX - 1,
            pltpu.roll(renewed, SUB - 1, 0),
            top[:, cut],
        )
    copies = [
        pltpu.make_async_copy(patch, out_ref.at[0, pl.ds(0, SUB), :], sems.at[0]),
        pltpu.make_async_copy(heat_ref, heat_hbm, sems.at[1]),
    ]
    for copy in copies:
        copy.start()
    for copy in copies:
        copy.wait()


def interval(
    sizes,
    thermal_anomaly,
    right_face_transport_ratio,
    species_ratios,
    lateral_spreading_number,
    depth_physics_operator,
    exchange_weight_table,
    sky_point_of_entry,
    water_indicator,
):
    sections, tile_count, lev_count = sizes
    _, levels, width = thermal_anomaly.shape
    tracers = species_ratios.shape[1]
    tiles = width // LANES
    rows = levels * tiles
    f32 = jnp.float32
    shape = jax.ShapeDtypeStruct
    flat = lambda x: x.reshape(rows, LANES)
    t, u, n = flat(thermal_anomaly), flat(right_face_transport_ratio), flat(lateral_spreading_number)
    q = jnp.transpose(species_ratios, (0, 2, 1, 3)).reshape(levels, tracers, width)
    lev = lax.axis_index("lev")

    group = 5 if levels % 5 == 0 else 1
    send_a, send_b, t_near, u_near, n_near, q_near = pl.pallas_call(
        functools.partial(edge_kernel, levels, tiles),
        out_shape=[shape((levels, LANES), f32)] * 2 + [shape((rows, LANES), f32)] * 3 + [shape((SUB, width), f32)],
        in_specs=[HBM] * 4,
        out_specs=[VMEM] * 6,
        scratch_shapes=[pltpu.SemaphoreType.DMA((4,))],
        compiler_params=PARAMS,
        name="edges",
    )(*(pltpu.with_memory_space_constraint(x, pltpu.HBM) for x in (t, u, n, q)))
    swap_a = [(i, i ^ 1) for i in range(tile_count)]
    swap_b = [(i, (i + 1) % tile_count if i % 2 else (i - 1) % tile_count) for i in range(tile_count)]
    got_a = lax.ppermute(send_a, "tile", swap_a)
    got_b = lax.ppermute(send_b, "tile", swap_b)
    pack = pl.pallas_call(
        functools.partial(pack_kernel, levels, tiles, group),
        out_shape=[shape((tracers, LANES), f32)] * 2,
        in_specs=[HBM],
        out_specs=[VMEM, VMEM],
        scratch_shapes=[pltpu.VMEM((levels, tracers, LANES), f32)] * 2
        + [pltpu.SemaphoreType.DMA((2, levels // group))],
        compiler_params=PARAMS,
        name="pack",
    )
    side_a, side_b = pack(pltpu.with_memory_space_constraint(q, pltpu.HBM))
    got_side_a = lax.ppermute(side_a, "tile", swap_a)
    got_side_b = lax.ppermute(side_b, "tile", swap_b)

    heating = pl.pallas_call(
        functools.partial(heat_kernel, levels, tiles, sections),
        out_shape=[shape((rows, LANES), f32), shape((5, levels, width), f32), shape((SUB, width), f32)],
        in_specs=[VMEM] * 6,
        out_specs=[VMEM] * 3,
        compiler_params=PARAMS,
        name="heat",
    )
    heat, coef, top = heating(t_near, u_near, n_near, q_near, got_a, got_b)

    others = [
        lax.ppermute(heat, "lev", [(i, peer(i, s, lev_count)) for i in range(lev_count)])
        for s in range(1, lev_count)
    ]

    index = sky_point_of_entry.T
    estimate = pl.CostEstimate(
        flops=9 * levels * tracers * width, bytes_accessed=4 * levels * tracers * width, transcendentals=0
    )
    inside = pl.pallas_call(
        functools.partial(inner_kernel, levels, tiles, tile_count),
        out_shape=[
            shape((levels, tracers, width), f32),
            shape((1, LANES), jnp.int32),
            shape(index.shape, jnp.int32),
            shape(index.shape, jnp.int32),
        ],
        in_specs=[VMEM] * 3,
        out_specs=[VMEM] * 4,
        cost_estimate=estimate,
        compiler_params=PARAMS,
        name="inside",
    )
    part, first, inner, outer = inside(q, coef, index)

    mine = lax.dynamic_slice_in_dim(depth_physics_operator[0], lev * levels, levels, 0)
    columns = [
        lax.dynamic_slice_in_dim(mine, source_of(lev, s, lev_count) * levels, levels, 1)
        for s in range(lev_count)
    ]
    matrix = jnp.concatenate(columns, axis=1)
    mixed, surface = pl.pallas_call(
        functools.partial(surface_kernel, levels, tiles, lev_count),
        out_shape=[shape((levels, width), f32), shape((tiles * NFLUX, LANES), f32)],
        in_specs=[VMEM] * (lev_count + 2),
        out_specs=[VMEM, VMEM],
        scratch_shapes=[pltpu.VMEM((levels * lev_count, width), f32)],
        compiler_params=PARAMS,
        name="surface",
    )(matrix, heat, *others, top)

    half = sections // 2
    place = lambda c, i, l: (c * tile_count + i) * lev_count + l

    def across(s):
        pairs = [
            (place(c, i, l), place((c + half) % sections, i ^ s, l))
            for c in range(sections)
            for i in range(tile_count)
            for l in range(lev_count)
        ]
        return lax.ppermute(surface, ("comp", "tile", "lev"), pairs)

    got = [None] * tile_count
    for s in range(1, tile_count, 2):
        got[s] = across(s)
    for s in range(1, tile_count, 2):
        got[s ^ 1] = lax.ppermute(got[s], "tile", swap_a)

    finish = pl.pallas_call(
        functools.partial(outer_kernel, levels, tiles, group),
        out_shape=shape((levels, tracers, width), f32),
        in_specs=[VMEM] * 5,
        out_specs=HBM,
        scratch_shapes=[pltpu.VMEM((levels, tracers, width), f32), pltpu.SemaphoreType.DMA((levels // group,))],
        cost_estimate=estimate,
        compiler_params=PARAMS,
        name="finish",
    )
    moved = finish(part, coef, got_side_a, got_side_b, mixed)

    heat_out, q_out = pl.pallas_call(
        functools.partial(final_kernel, levels, tiles, tile_count, sections),
        out_shape=[shape((rows, LANES), f32), shape((levels, tracers, width), f32)],
        in_specs=[VMEM] * (7 + tile_count) + [HBM],
        out_specs=[HBM, HBM],
        scratch_shapes=[
            pltpu.VMEM((tile_count * tiles * SUB, LANES), f32),
            pltpu.VMEM((SUB, width), f32),
            pltpu.VMEM((rows, LANES), f32),
            pltpu.SemaphoreType.DMA((2,)),
        ],
        input_output_aliases={7 + tile_count: 1},
        compiler_params=PARAMS,
        name="remap",
    )(
        first, inner, outer, mixed, top, exchange_weight_table.T, water_indicator.reshape(1, width), *got, moved
    )
    thermal_anomaly_ending = heat_out.reshape(1, levels, width)
    species_ratios_ending = jnp.transpose(q_out.reshape(1, levels, tracers, width), (0, 2, 1, 3))
    return thermal_anomaly_ending, species_ratios_ending


def solution(mesh):
    in_specs = (
        P("comp", "lev", "tile"),
        P("comp", "lev", "tile"),
        P("comp", None, "lev", "tile"),
        P("comp", "lev", "tile"),
        P("comp", None, None),
        P("tile", None),
        P("tile", None),
        P("tile"),
    )
    out_specs = (P("comp", "lev", "tile"), P("comp", None, "lev", "tile"))
    sizes = (mesh.shape["comp"], mesh.shape["tile"], mesh.shape["lev"])
    return jax.shard_map(
        functools.partial(interval, sizes), mesh=mesh, in_specs=in_specs, out_specs=out_specs, check_vma=False
    )
```

```python
import functools

import jax
import jax.numpy as jnp
from jax import lax
from jax.experimental import pallas as pl
from jax.experimental.pallas import tpu as pltpu
from jax.sharding import PartitionSpec as P


NFLUX = 4
LANES = 128
SUB = 8
REACH = 128
T_AT, U_AT, N_AT = LANES - 6, LANES - 4, LANES - 2

VMEM = pl.BlockSpec(memory_space=pltpu.VMEM)
SMEM = pl.BlockSpec(memory_space=pltpu.SMEM)
HBM = pl.BlockSpec(memory_space=pltpu.HBM)
PARAMS = pltpu.CompilerParams(vmem_limit_bytes=8 * 2**20)


def peer(i, s, n):
    return i ^ s if n & (n - 1) == 0 else (i + s) % n


def source_of(me, s, n):
    return me ^ s if n & (n - 1) == 0 else lax.rem(me - s + n, n)


def lane_iota(shape):
    return lax.broadcasted_iota(jnp.int32, shape, len(shape) - 1)


def wide(ref, levels, tiles):
    return jnp.concatenate([ref[pl.ds(t, levels, stride=tiles), :] for t in range(tiles)], axis=1)


def from_left(x, k, halo, place):
    moved = pltpu.roll(x, k, 1)
    edge = pltpu.roll(halo, (k - place - 2) % LANES, 1)
    head = jnp.where(lane_iota(edge.shape) < k, edge, moved[:, :LANES])
    return jnp.concatenate([head, moved[:, LANES:]], axis=1)


def from_right(x, k, halo, place):
    width = x.shape[1]
    moved = pltpu.roll(x, width - k, 1)
    edge = pltpu.roll(halo, (-k - place) % LANES, 1)
    tail = jnp.where(lane_iota(edge.shape) >= LANES - k, edge, moved[:, width - LANES :])
    return jnp.concatenate([moved[:, : width - LANES], tail], axis=1)


def edge_kernel(
    levels, tiles, t_hbm, u_hbm, n_hbm, q_hbm, a_ref, b_ref, t_ref, u_ref, n_ref, top_ref, sems
):
    copies = [
        pltpu.make_async_copy(source, target, sems.at[i])
        for i, (source, target) in enumerate(
            ((t_hbm, t_ref), (u_hbm, u_ref), (n_hbm, n_ref), (q_hbm.at[0, pl.ds(0, SUB), :], top_ref))
        )
    ]
    for copy in copies:
        copy.start()
    even = lax.rem(lax.axis_index("tile"), 2) == 0
    lane = lane_iota((levels, LANES))

    def small(tile, edge):
        t, u, n = [
            pltpu.roll(r[pl.ds(tile, levels, stride=tiles), :], (at - edge) % LANES, 1)
            for r, at in ((t_ref, T_AT), (u_ref, U_AT), (n_ref, N_AT))
        ]
        top = pltpu.roll(top_ref[:, tile * LANES : (tile + 1) * LANES], -edge % LANES, 1)
        top = jnp.concatenate([top, jnp.zeros((levels - SUB, LANES), jnp.float32)], axis=0)
        return jnp.where(lane < 2, top, jnp.where(lane < U_AT, t, jnp.where(lane < N_AT, u, n)))

    for copy in copies:
        copy.wait()
    left = small(0, 0)
    right = small(tiles - 1, LANES - 2)
    a_ref[...] = jnp.where(even, right, left)
    b_ref[...] = jnp.where(even, left, right)


def pack_kernel(levels, tiles, group, q_hbm, a_ref, b_ref, left, right, sems):
    width = tiles * LANES
    chunks = []
    for g in range(levels // group):
        cut = pl.ds(g * group, group)
        chunks.append(
            [
                pltpu.make_async_copy(q_hbm.at[cut, :, pl.ds(0, LANES)], left.at[cut], sems.at[0, g]),
                pltpu.make_async_copy(q_hbm.at[cut, :, pl.ds(width - LANES, LANES)], right.at[cut], sems.at[1, g]),
            ]
        )
        for copy in chunks[-1]:
            copy.start()
    even = lax.rem(lax.axis_index("tile"), 2) == 0
    tracers = a_ref.shape[0]
    pair = lane_iota((tracers, LANES)) // 2
    packed_left = packed_right = jnp.zeros((tracers, LANES), jnp.float32)
    for g, chunk in enumerate(chunks):
        for copy in chunk:
            copy.wait()
        for level in range(g * group, (g + 1) * group):
            here = pair == level
            packed_left = jnp.where(here, pltpu.roll(left[level], 2 * level, 1), packed_left)
            packed_right = jnp.where(here, pltpu.roll(right[level], (2 * level + 2) % LANES, 1), packed_right)
    a_ref[...] = jnp.where(even, packed_right, packed_left)
    b_ref[...] = jnp.where(even, packed_left, packed_right)


def heat_kernel(levels, tiles, sections, t_ref, u_ref, n_ref, near_ref, a_ref, b_ref, heat_ref, coef_ref, top_ref):
    even = lax.rem(lax.axis_index("tile"), 2) == 0
    ocean = lax.axis_index("comp") >= sections // 2
    t, u, n = [wide(r, levels, tiles) for r in (t_ref, u_ref, n_ref)]
    low = jnp.where(even, b_ref[...], a_ref[...])
    high = jnp.where(even, a_ref[...], b_ref[...])
    ul1, ul2 = [from_left(u, k, low, U_AT) for k in (1, 2)]
    ur1 = from_right(u, 1, high, U_AT)
    plus = lambda v: jnp.maximum(v, 0.0)
    minus = lambda v: jnp.minimum(v, 0.0)
    a0, b0, c0 = 1.0 - plus(u) + minus(ul1), plus(ul1), -minus(u)
    am, bm, cm = 1.0 - plus(ul1) + minus(ul2), plus(ul2), -minus(ul1)
    ap, bp, cp = 1.0 - plus(ur1) + minus(u), plus(u), -minus(ur1)

    def composed(a0, b0, c0, am, bm, cm, ap, bp, cp):
        return (
            jnp.where(ocean, a0, a0 * a0 + b0 * cm + c0 * bp),
            jnp.where(ocean, b0, b0 * (a0 + am)),
            jnp.where(ocean, c0, c0 * (a0 + ap)),
            jnp.where(ocean, 0.0, b0 * bm),
            jnp.where(ocean, 0.0, c0 * cp),
        )

    shared = composed(a0, b0, c0, am, bm, cm, ap, bp, cp)
    for k, value in enumerate(shared):
        coef_ref[k] = value
    q = near_ref[...]
    f0, f1, f2, f3, f4 = [value[0:1] for value in shared]
    top_low, top_high = low[:SUB], high[:SUB]
    top_ref[...] = (
        f0 * q
        + f1 * from_left(q, 1, top_low, 0)
        + f2 * from_right(q, 1, top_high, 0)
        + f3 * from_left(q, 2, top_low, 0)
        + f4 * from_right(q, 2, top_high, 0)
    )
    nl = from_left(n, 1, low, N_AT)
    nr = from_right(n, 1, high, N_AT)
    e0, e1, e2, e3, e4 = composed(
        a0 - 2.0 * n, b0 + n, c0 + n, am - 2.0 * nl, bm + nl, cm + nl, ap - 2.0 * nr, bp + nr, cp + nr
    )
    tl1, tl2 = [from_left(t, k, low, T_AT) for k in (1, 2)]
    tr1, tr2 = [from_right(t, k, high, T_AT) for k in (1, 2)]
    heat = e0 * t + e1 * tl1 + e2 * tr1 + e3 * tl2 + e4 * tr2
    for tile in range(tiles):
        heat_ref[pl.ds(tile, levels, stride=tiles), :] = heat[:, tile * LANES : (tile + 1) * LANES]


def plan(tiles, count, first_ref, index_ref, inner_ref, outer_ref):
    cells = count * tiles * LANES
    index = index_ref[...]
    lane = lane_iota(index.shape)
    at = index - (first_ref[0] * LANES - REACH) - lane
    at = jnp.where(at < 0, at + cells, at)
    at = jnp.where(at >= cells, at - cells, at) + jnp.bitwise_and(lane, LANES - 1)
    inner_ref[...] = jnp.bitwise_and(at, LANES - 1)
    outer_ref[...] = jnp.right_shift(at, 7)


def inner_kernel(
    levels, tiles, count, first_ref, q_ref, coef_ref, index_ref, new_ref, inner_ref, outer_ref
):
    plan(tiles, count, first_ref, index_ref, inner_ref, outer_ref)
    none = jnp.zeros((q_ref.shape[1], LANES), jnp.float32)
    for level in range(levels):
        q = q_ref[level]
        e0, e1, e2, e3, e4 = [coef_ref[k, level : level + 1, :] for k in range(5)]
        new_ref[level] = (
            e0 * q
            + e1 * from_left(q, 1, none, 0)
            + e2 * from_right(q, 1, none, 0)
            + e3 * from_left(q, 2, none, 0)
            + e4 * from_right(q, 2, none, 0)
        )


def outer_kernel(levels, tiles, group, part_ref, coef_ref, a_ref, b_ref, after_ref, out_hbm, new_ref, sems):
    del after_ref
    even = lax.rem(lax.axis_index("tile"), 2) == 0
    low = jnp.where(even, b_ref[...], a_ref[...])
    high = jnp.where(even, a_ref[...], b_ref[...])
    lane = lane_iota(low.shape)
    head, last = slice(0, LANES), slice((tiles - 1) * LANES, tiles * LANES)
    copies = []
    for level in range(levels):
        new_ref[level] = part_ref[level]
        added = jnp.zeros(low.shape, jnp.float32)
        for k, e in ((1, 1), (2, 3)):
            halo = pltpu.roll(low, (k - 2 * level - 2) % LANES, 1)
            added = added + coef_ref[e, level : level + 1, head] * jnp.where(lane < k, halo, 0.0)
        new_ref[level, :, head] = part_ref[level, :, head] + added
        added = jnp.zeros(low.shape, jnp.float32)
        for k, e in ((1, 2), (2, 4)):
            halo = pltpu.roll(high, (-k - 2 * level) % LANES, 1)
            added = added + coef_ref[e, level : level + 1, last] * jnp.where(lane >= LANES - k, halo, 0.0)
        new_ref[level, :, last] = (new_ref if tiles == 1 else part_ref)[level, :, last] + added
        if level % group == group - 1:
            cut = pl.ds(level - group + 1, group)
            copies.append(pltpu.make_async_copy(new_ref.at[cut], out_hbm.at[cut], sems.at[level // group]))
            copies[-1].start()
    for copy in copies:
        copy.wait()


def surface_kernel(levels, tiles, count, m_ref, own_ref, *refs):
    got, (top_ref, mixed_ref, send_ref, whole) = refs[: count - 1], refs[count - 1 :]
    for s, ref in enumerate((own_ref,) + tuple(got)):
        whole[pl.ds(s * levels, levels), :] = wide(ref, levels, tiles)
    mixed = jnp.dot(
        m_ref[...], whole[...], precision=lax.Precision.HIGHEST, preferred_element_type=jnp.float32
    )
    mixed_ref[...] = mixed
    fields = jnp.where(
        lax.broadcasted_iota(jnp.int32, (SUB, tiles * LANES), 0) == 0,
        jnp.broadcast_to(mixed[0:1], (SUB, tiles * LANES)),
        pltpu.roll(top_ref[...], 1, 0),
    )
    for tile in range(tiles):
        send_ref[pl.ds(tile * NFLUX, NFLUX), :] = fields[:NFLUX, tile * LANES : (tile + 1) * LANES]


def final_kernel(
    levels, tiles, count, sections, first_ref, inner_ref, outer_ref, mixed_ref, top_ref, weight_ref, water_ref, *refs
):
    got, (q_ref, heat_hbm, out_ref, whole, patch, heat_ref, sems) = refs[:count], refs[count:]
    del q_ref
    here = lax.axis_index("tile")
    sea = jnp.logical_and(
        lax.axis_index("comp") >= sections // 2, lax.axis_index("lev") == 0
    )
    for s in range(count):
        base = (here ^ s) * tiles * SUB
        for tile in range(tiles):
            whole[pl.ds(pl.multiple_of(base + tile * SUB, SUB), NFLUX), :] = got[s][pl.ds(tile * NFLUX, NFLUX), :]
    first = first_ref[0]
    top = top_ref[...]
    mixed = mixed_ref[...]
    first_row = lax.broadcasted_iota(jnp.int32, (SUB, LANES), 0) == 0
    lane = lane_iota((SUB, LANES))
    for tile in range(tiles):
        cut = slice(tile * LANES, (tile + 1) * LANES)
        windows = []
        for q in range(3):
            block = lax.rem(first + tile + q - 1 + count * tiles, count * tiles)
            windows.append(whole[pl.ds(pl.multiple_of(block * SUB, SUB), SUB), :])
        total = jnp.zeros((SUB, LANES), jnp.float32)
        for k in range(weight_ref.shape[0]):
            weight = jnp.broadcast_to(weight_ref[k : k + 1, cut], (SUB, LANES))
            inner = jnp.broadcast_to(inner_ref[k : k + 1, cut], (SUB, LANES))
            outer = jnp.broadcast_to(outer_ref[k : k + 1, cut], (SUB, LANES))
            picks = [jnp.take_along_axis(w, inner, axis=1) for w in windows]
            picked = jnp.where(outer == 0, picks[0], jnp.where(outer == 1, picks[1], picks[2]))
            total = total + picked * weight
        own_heat = jnp.broadcast_to(mixed[0:1, cut], (SUB, LANES))
        surface = jnp.where(first_row, own_heat, pltpu.roll(top[:, cut], 1, 0))
        wet = jnp.logical_and(sea, jnp.broadcast_to(water_ref[0:1, cut], (SUB, LANES)) == 1)
        wet = jnp.logical_and(wet, lax.broadcasted_iota(jnp.int32, (SUB, LANES), 0) < NFLUX)
        renewed = jnp.where(wet, surface + 0.5 * (total - surface), surface)
        heat_ref[pl.ds(tile, levels, stride=tiles), :] = mixed[:, cut]
        heat_ref[pl.ds(tile, 1), :] = renewed[0:1]
        patch[:, cut] = jnp.where(
            lax.broadcasted_iota(jnp.int32, (SUB, LANES), 0) < NFLUX - 1,
            pltpu.roll(renewed, SUB - 1, 0),
            top[:, cut],
        )
    copies = [
        pltpu.make_async_copy(patch, out_ref.at[0, pl.ds(0, SUB), :], sems.at[0]),
        pltpu.make_async_copy(heat_ref, heat_hbm, sems.at[1]),
    ]
    for copy in copies:
        copy.start()
    for copy in copies:
        copy.wait()


def interval(
    sizes,
    thermal_anomaly,
    right_face_transport_ratio,
    species_ratios,
    lateral_spreading_number,
    depth_physics_operator,
    exchange_weight_table,
    sky_point_of_entry,
    water_indicator,
):
    sections, tile_count, lev_count = sizes
    _, levels, width = thermal_anomaly.shape
    tracers = species_ratios.shape[1]
    tiles = width // LANES
    rows = levels * tiles
    f32 = jnp.float32
    shape = jax.ShapeDtypeStruct
    flat = lambda x: x.reshape(rows, LANES)
    t, u, n = flat(thermal_anomaly), flat(right_face_transport_ratio), flat(lateral_spreading_number)
    q = jnp.transpose(species_ratios, (0, 2, 1, 3)).reshape(levels, tracers, width)
    lev = lax.axis_index("lev")

    group = 5 if levels % 5 == 0 else 1
    send_a, send_b, t_near, u_near, n_near, q_near = pl.pallas_call(
        functools.partial(edge_kernel, levels, tiles),
        out_shape=[shape((levels, LANES), f32)] * 2 + [shape((rows, LANES), f32)] * 3 + [shape((SUB, width), f32)],
        in_specs=[HBM] * 4,
        out_specs=[VMEM] * 6,
        scratch_shapes=[pltpu.SemaphoreType.DMA((4,))],
        compiler_params=PARAMS,
        name="edges",
    )(*(pltpu.with_memory_space_constraint(x, pltpu.HBM) for x in (t, u, n, q)))
    swap_a = [(i, i ^ 1) for i in range(tile_count)]
    swap_b = [(i, (i + 1) % tile_count if i % 2 else (i - 1) % tile_count) for i in range(tile_count)]
    got_a = lax.ppermute(send_a, "tile", swap_a)
    got_b = lax.ppermute(send_b, "tile", swap_b)
    pack = pl.pallas_call(
        functools.partial(pack_kernel, levels, tiles, group),
        out_shape=[shape((tracers, LANES), f32)] * 2,
        in_specs=[HBM],
        out_specs=[VMEM, VMEM],
        scratch_shapes=[pltpu.VMEM((levels, tracers, LANES), f32)] * 2
        + [pltpu.SemaphoreType.DMA((2, levels // group))],
        compiler_params=PARAMS,
        name="pack",
    )
    side_a, side_b = pack(pltpu.with_memory_space_constraint(q, pltpu.HBM))
    got_side_a = lax.ppermute(side_a, "tile", swap_a)
    got_side_b = lax.ppermute(side_b, "tile", swap_b)

    heating = pl.pallas_call(
        functools.partial(heat_kernel, levels, tiles, sections),
        out_shape=[shape((rows, LANES), f32), shape((5, levels, width), f32), shape((SUB, width), f32)],
        in_specs=[VMEM] * 6,
        out_specs=[VMEM] * 3,
        compiler_params=PARAMS,
        name="heat",
    )
    heat, coef, top = heating(t_near, u_near, n_near, q_near, got_a, got_b)

    others = [
        lax.ppermute(heat, "lev", [(i, peer(i, s, lev_count)) for i in range(lev_count)])
        for s in range(1, lev_count)
    ]

    index = sky_point_of_entry.T
    first = ((index[0, 0:1] + REACH) % (tile_count * width)) // width * tiles
    estimate = pl.CostEstimate(
        flops=9 * levels * tracers * width, bytes_accessed=4 * levels * tracers * width, transcendentals=0
    )
    inside = pl.pallas_call(
        functools.partial(inner_kernel, levels, tiles, tile_count),
        out_shape=[
            shape((levels, tracers, width), f32),
            shape(index.shape, jnp.int32),
            shape(index.shape, jnp.int32),
        ],
        in_specs=[SMEM] + [VMEM] * 3,
        out_specs=[VMEM] * 3,
        cost_estimate=estimate,
        compiler_params=PARAMS,
        name="inside",
    )
    part, inner, outer = inside(first, q, coef, index)

    operator, _ = lax.optimization_barrier((depth_physics_operator, heat))
    mine = lax.dynamic_slice_in_dim(operator[0], lev * levels, levels, 0)
    columns = [
        lax.dynamic_slice_in_dim(mine, source_of(lev, s, lev_count) * levels, levels, 1)
        for s in range(lev_count)
    ]
    matrix = jnp.concatenate(columns, axis=1)
    mixed, surface = pl.pallas_call(
        functools.partial(surface_kernel, levels, tiles, lev_count),
        out_shape=[shape((levels, width), f32), shape((tiles * NFLUX, LANES), f32)],
        in_specs=[VMEM] * (lev_count + 2),
        out_specs=[VMEM, VMEM],
        scratch_shapes=[pltpu.VMEM((levels * lev_count, width), f32)],
        compiler_params=PARAMS,
        name="surface",
    )(matrix, heat, *others, top)

    half = sections // 2
    place = lambda c, i, l: (c * tile_count + i) * lev_count + l

    def across(s):
        pairs = [
            (place(c, i, l), place((c + half) % sections, i ^ s, l))
            for c in range(sections)
            for i in range(tile_count)
            for l in range(lev_count)
        ]
        return lax.ppermute(surface, ("comp", "tile", "lev"), pairs)

    got = [None] * tile_count
    for s in range(1, tile_count, 2):
        got[s] = across(s)
    for s in range(1, tile_count, 2):
        got[s ^ 1] = lax.ppermute(got[s], "tile", swap_a)

    finish = pl.pallas_call(
        functools.partial(outer_kernel, levels, tiles, group),
        out_shape=shape((levels, tracers, width), f32),
        in_specs=[VMEM] * 5,
        out_specs=HBM,
        scratch_shapes=[pltpu.VMEM((levels, tracers, width), f32), pltpu.SemaphoreType.DMA((levels // group,))],
        cost_estimate=estimate,
        compiler_params=PARAMS,
        name="finish",
    )
    moved = finish(part, coef, got_side_a, got_side_b, mixed)

    heat_out, q_out = pl.pallas_call(
        functools.partial(final_kernel, levels, tiles, tile_count, sections),
        out_shape=[shape((rows, LANES), f32), shape((levels, tracers, width), f32)],
        in_specs=[SMEM] + [VMEM] * (6 + tile_count) + [HBM],
        out_specs=[HBM, HBM],
        scratch_shapes=[
            pltpu.VMEM((tile_count * tiles * SUB, LANES), f32),
            pltpu.VMEM((SUB, width), f32),
            pltpu.VMEM((rows, LANES), f32),
            pltpu.SemaphoreType.DMA((2,)),
        ],
        input_output_aliases={7 + tile_count: 1},
        compiler_params=PARAMS,
        name="remap",
    )(
        first, inner, outer, mixed, top, exchange_weight_table.T, water_indicator.reshape(1, width), *got, moved
    )
    thermal_anomaly_ending = heat_out.reshape(1, levels, width)
    species_ratios_ending = jnp.transpose(q_out.reshape(1, levels, tracers, width), (0, 2, 1, 3))
    return thermal_anomaly_ending, species_ratios_ending


def solution(mesh):
    in_specs = (
        P("comp", "lev", "tile"),
        P("comp", "lev", "tile"),
        P("comp", None, "lev", "tile"),
        P("comp", "lev", "tile"),
        P("comp", None, None),
        P("tile", None),
        P("tile", None),
        P("tile"),
    )
    out_specs = (P("comp", "lev", "tile"), P("comp", None, "lev", "tile"))
    sizes = (mesh.shape["comp"], mesh.shape["tile"], mesh.shape["lev"])
    return jax.shard_map(
        functools.partial(interval, sizes), mesh=mesh, in_specs=in_specs, out_specs=out_specs, check_vma=False
    )
```

```python
import functools

import jax
import jax.numpy as jnp
from jax import lax
from jax.experimental import pallas as pl
from jax.experimental.pallas import tpu as pltpu
from jax.sharding import PartitionSpec as P


NFLUX = 4
LANES = 128
SUB = 8
REACH = 128
T_AT, U_AT, N_AT = LANES - 6, LANES - 4, LANES - 2

VMEM = pl.BlockSpec(memory_space=pltpu.VMEM)
SMEM = pl.BlockSpec(memory_space=pltpu.SMEM)
HBM = pl.BlockSpec(memory_space=pltpu.HBM)
PARAMS = pltpu.CompilerParams(vmem_limit_bytes=8 * 2**20)


def peer(i, s, n):
    return i ^ s if n & (n - 1) == 0 else (i + s) % n


def source_of(me, s, n):
    return me ^ s if n & (n - 1) == 0 else lax.rem(me - s + n, n)


def lane_iota(shape):
    return lax.broadcasted_iota(jnp.int32, shape, len(shape) - 1)


def wide(ref, levels, tiles):
    return jnp.concatenate([ref[pl.ds(t, levels, stride=tiles), :] for t in range(tiles)], axis=1)


def from_left(x, k, halo, place):
    moved = pltpu.roll(x, k, 1)
    edge = pltpu.roll(halo, (k - place - 2) % LANES, 1)
    head = jnp.where(lane_iota(edge.shape) < k, edge, moved[:, :LANES])
    return jnp.concatenate([head, moved[:, LANES:]], axis=1)


def from_right(x, k, halo, place):
    width = x.shape[1]
    moved = pltpu.roll(x, width - k, 1)
    edge = pltpu.roll(halo, (-k - place) % LANES, 1)
    tail = jnp.where(lane_iota(edge.shape) >= LANES - k, edge, moved[:, width - LANES :])
    return jnp.concatenate([moved[:, : width - LANES], tail], axis=1)


def edge_kernel(
    levels, tiles, t_hbm, u_hbm, n_hbm, q_hbm, a_ref, b_ref, t_ref, u_ref, n_ref, top_ref, sems
):
    copies = [
        pltpu.make_async_copy(source, target, sems.at[i])
        for i, (source, target) in enumerate(
            ((t_hbm, t_ref), (u_hbm, u_ref), (n_hbm, n_ref), (q_hbm.at[0, pl.ds(0, SUB), :], top_ref))
        )
    ]
    for copy in copies:
        copy.start()
    even = lax.rem(lax.axis_index("tile"), 2) == 0
    lane = lane_iota((levels, LANES))

    def small(tile, edge):
        t, u, n = [
            pltpu.roll(r[pl.ds(tile, levels, stride=tiles), :], (at - edge) % LANES, 1)
            for r, at in ((t_ref, T_AT), (u_ref, U_AT), (n_ref, N_AT))
        ]
        top = pltpu.roll(top_ref[:, tile * LANES : (tile + 1) * LANES], -edge % LANES, 1)
        top = jnp.concatenate([top, jnp.zeros((levels - SUB, LANES), jnp.float32)], axis=0)
        return jnp.where(lane < 2, top, jnp.where(lane < U_AT, t, jnp.where(lane < N_AT, u, n)))

    for copy in copies:
        copy.wait()
    left = small(0, 0)
    right = small(tiles - 1, LANES - 2)
    a_ref[...] = jnp.where(even, right, left)
    b_ref[...] = jnp.where(even, left, right)


def pack_kernel(levels, tiles, group, q_hbm, a_ref, b_ref, left, right, sems):
    width = tiles * LANES
    chunks = []
    for g in range(levels // group):
        cut = pl.ds(g * group, group)
        chunks.append(
            [
                pltpu.make_async_copy(q_hbm.at[cut, :, pl.ds(0, LANES)], left.at[cut], sems.at[0, g]),
                pltpu.make_async_copy(q_hbm.at[cut, :, pl.ds(width - LANES, LANES)], right.at[cut], sems.at[1, g]),
            ]
        )
        for copy in chunks[-1]:
            copy.start()
    even = lax.rem(lax.axis_index("tile"), 2) == 0
    tracers = a_ref.shape[0]
    pair = lane_iota((tracers, LANES)) // 2
    packed_left = packed_right = jnp.zeros((tracers, LANES), jnp.float32)
    for g, chunk in enumerate(chunks):
        for copy in chunk:
            copy.wait()
        for level in range(g * group, (g + 1) * group):
            here = pair == level
            packed_left = jnp.where(here, pltpu.roll(left[level], 2 * level, 1), packed_left)
            packed_right = jnp.where(here, pltpu.roll(right[level], (2 * level + 2) % LANES, 1), packed_right)
    a_ref[...] = jnp.where(even, packed_right, packed_left)
    b_ref[...] = jnp.where(even, packed_left, packed_right)


def heat_kernel(levels, tiles, sections, t_ref, u_ref, n_ref, near_ref, a_ref, b_ref, heat_ref, coef_ref, top_ref):
    even = lax.rem(lax.axis_index("tile"), 2) == 0
    ocean = lax.axis_index("comp") >= sections // 2
    t, u, n = [wide(r, levels, tiles) for r in (t_ref, u_ref, n_ref)]
    low = jnp.where(even, b_ref[...], a_ref[...])
    high = jnp.where(even, a_ref[...], b_ref[...])
    ul1, ul2 = [from_left(u, k, low, U_AT) for k in (1, 2)]
    ur1 = from_right(u, 1, high, U_AT)
    plus = lambda v: jnp.maximum(v, 0.0)
    minus = lambda v: jnp.minimum(v, 0.0)
    a0, b0, c0 = 1.0 - plus(u) + minus(ul1), plus(ul1), -minus(u)
    am, bm, cm = 1.0 - plus(ul1) + minus(ul2), plus(ul2), -minus(ul1)
    ap, bp, cp = 1.0 - plus(ur1) + minus(u), plus(u), -minus(ur1)

    def composed(a0, b0, c0, am, bm, cm, ap, bp, cp):
        return (
            jnp.where(ocean, a0, a0 * a0 + b0 * cm + c0 * bp),
            jnp.where(ocean, b0, b0 * (a0 + am)),
            jnp.where(ocean, c0, c0 * (a0 + ap)),
            jnp.where(ocean, 0.0, b0 * bm),
            jnp.where(ocean, 0.0, c0 * cp),
        )

    shared = composed(a0, b0, c0, am, bm, cm, ap, bp, cp)
    for k, value in enumerate(shared):
        coef_ref[k] = value
    q = near_ref[...]
    f0, f1, f2, f3, f4 = [value[0:1] for value in shared]
    top_low, top_high = low[:SUB], high[:SUB]
    top_ref[...] = (
        f0 * q
        + f1 * from_left(q, 1, top_low, 0)
        + f2 * from_right(q, 1, top_high, 0)
        + f3 * from_left(q, 2, top_low, 0)
        + f4 * from_right(q, 2, top_high, 0)
    )
    nl = from_left(n, 1, low, N_AT)
    nr = from_right(n, 1, high, N_AT)
    e0, e1, e2, e3, e4 = composed(
        a0 - 2.0 * n, b0 + n, c0 + n, am - 2.0 * nl, bm + nl, cm + nl, ap - 2.0 * nr, bp + nr, cp + nr
    )
    tl1, tl2 = [from_left(t, k, low, T_AT) for k in (1, 2)]
    tr1, tr2 = [from_right(t, k, high, T_AT) for k in (1, 2)]
    heat = e0 * t + e1 * tl1 + e2 * tr1 + e3 * tl2 + e4 * tr2
    for tile in range(tiles):
        heat_ref[pl.ds(tile, levels, stride=tiles), :] = heat[:, tile * LANES : (tile + 1) * LANES]


def plan(tiles, count, first_ref, index_ref, inner_ref, outer_ref):
    cells = count * tiles * LANES
    index = index_ref[...]
    lane = lane_iota(index.shape)
    at = index - (first_ref[0] * LANES - REACH) - lane
    at = jnp.where(at < 0, at + cells, at)
    at = jnp.where(at >= cells, at - cells, at) + jnp.bitwise_and(lane, LANES - 1)
    inner_ref[...] = jnp.bitwise_and(at, LANES - 1)
    outer_ref[...] = jnp.right_shift(at, 7)


def inner_kernel(
    levels, tiles, count, first_ref, q_ref, coef_ref, index_ref, new_ref, inner_ref, outer_ref
):
    plan(tiles, count, first_ref, index_ref, inner_ref, outer_ref)
    none = jnp.zeros((q_ref.shape[1], LANES), jnp.float32)
    for level in range(levels):
        q = q_ref[level]
        e0, e1, e2, e3, e4 = [coef_ref[k, level : level + 1, :] for k in range(5)]
        new_ref[level] = (
            e0 * q
            + e1 * from_left(q, 1, none, 0)
            + e2 * from_right(q, 1, none, 0)
            + e3 * from_left(q, 2, none, 0)
            + e4 * from_right(q, 2, none, 0)
        )


def outer_kernel(levels, tiles, group, part_ref, coef_ref, a_ref, b_ref, after_ref, out_hbm, new_ref, sems):
    del after_ref
    even = lax.rem(lax.axis_index("tile"), 2) == 0
    low = jnp.where(even, b_ref[...], a_ref[...])
    high = jnp.where(even, a_ref[...], b_ref[...])
    lane = lane_iota(low.shape)
    head, last = slice(0, LANES), slice((tiles - 1) * LANES, tiles * LANES)
    copies = []
    for level in range(levels):
        new_ref[level] = part_ref[level]
        added = jnp.zeros(low.shape, jnp.float32)
        for k, e in ((1, 1), (2, 3)):
            halo = pltpu.roll(low, (k - 2 * level - 2) % LANES, 1)
            added = added + coef_ref[e, level : level + 1, head] * jnp.where(lane < k, halo, 0.0)
        new_ref[level, :, head] = part_ref[level, :, head] + added
        added = jnp.zeros(low.shape, jnp.float32)
        for k, e in ((1, 2), (2, 4)):
            halo = pltpu.roll(high, (-k - 2 * level) % LANES, 1)
            added = added + coef_ref[e, level : level + 1, last] * jnp.where(lane >= LANES - k, halo, 0.0)
        new_ref[level, :, last] = (new_ref if tiles == 1 else part_ref)[level, :, last] + added
        if level % group == group - 1:
            cut = pl.ds(level - group + 1, group)
            copies.append(pltpu.make_async_copy(new_ref.at[cut], out_hbm.at[cut], sems.at[level // group]))
            copies[-1].start()
    for copy in copies:
        copy.wait()


def surface_kernel(levels, tiles, count, m_ref, own_ref, *refs):
    got, (top_ref, mixed_ref, send_ref, whole) = refs[: count - 1], refs[count - 1 :]
    for s, ref in enumerate((own_ref,) + tuple(got)):
        whole[pl.ds(s * levels, levels), :] = wide(ref, levels, tiles)
    mixed = jnp.dot(
        m_ref[...], whole[...], precision=lax.Precision.HIGHEST, preferred_element_type=jnp.float32
    )
    mixed_ref[...] = mixed
    fields = jnp.where(
        lax.broadcasted_iota(jnp.int32, (SUB, tiles * LANES), 0) == 0,
        jnp.broadcast_to(mixed[0:1], (SUB, tiles * LANES)),
        pltpu.roll(top_ref[...], 1, 0),
    )
    for tile in range(tiles):
        send_ref[pl.ds(tile * NFLUX, NFLUX), :] = fields[:NFLUX, tile * LANES : (tile + 1) * LANES]


def final_kernel(
    levels, tiles, count, sections, first_ref, inner_ref, outer_ref, mixed_ref, top_ref, weight_ref, water_ref, *refs
):
    joined_ref, shared_ref, q_ref, heat_hbm, out_ref, whole, patch, heat_ref, sems = refs
    del q_ref
    here = lax.axis_index("tile")
    sea = jnp.logical_and(
        lax.axis_index("comp") >= sections // 2, lax.axis_index("lev") == 0
    )
    for s in range(count):
        base = (here ^ s) * tiles * SUB
        for tile in range(tiles):
            row = (s // 2 * tiles + tile) * NFLUX
            got = joined_ref if s % 2 else shared_ref
            whole[pl.ds(pl.multiple_of(base + tile * SUB, SUB), NFLUX), :] = got[pl.ds(row, NFLUX), :]
    first = first_ref[0]
    top = top_ref[...]
    mixed = mixed_ref[...]
    first_row = lax.broadcasted_iota(jnp.int32, (SUB, LANES), 0) == 0
    lane = lane_iota((SUB, LANES))
    for tile in range(tiles):
        cut = slice(tile * LANES, (tile + 1) * LANES)
        windows = []
        for q in range(3):
            block = lax.rem(first + tile + q - 1 + count * tiles, count * tiles)
            windows.append(whole[pl.ds(pl.multiple_of(block * SUB, SUB), SUB), :])
        total = jnp.zeros((SUB, LANES), jnp.float32)
        for k in range(weight_ref.shape[0]):
            weight = jnp.broadcast_to(weight_ref[k : k + 1, cut], (SUB, LANES))
            inner = jnp.broadcast_to(inner_ref[k : k + 1, cut], (SUB, LANES))
            outer = jnp.broadcast_to(outer_ref[k : k + 1, cut], (SUB, LANES))
            picks = [jnp.take_along_axis(w, inner, axis=1) for w in windows]
            picked = jnp.where(outer == 0, picks[0], jnp.where(outer == 1, picks[1], picks[2]))
            total = total + picked * weight
        own_heat = jnp.broadcast_to(mixed[0:1, cut], (SUB, LANES))
        surface = jnp.where(first_row, own_heat, pltpu.roll(top[:, cut], 1, 0))
        wet = jnp.logical_and(sea, jnp.broadcast_to(water_ref[0:1, cut], (SUB, LANES)) == 1)
        wet = jnp.logical_and(wet, lax.broadcasted_iota(jnp.int32, (SUB, LANES), 0) < NFLUX)
        renewed = jnp.where(wet, surface + 0.5 * (total - surface), surface)
        heat_ref[pl.ds(tile, levels, stride=tiles), :] = mixed[:, cut]
        heat_ref[pl.ds(tile, 1), :] = renewed[0:1]
        patch[:, cut] = jnp.where(
            lax.broadcasted_iota(jnp.int32, (SUB, LANES), 0) < NFLUX - 1,
            pltpu.roll(renewed, SUB - 1, 0),
            top[:, cut],
        )
    copies = [
        pltpu.make_async_copy(patch, out_ref.at[0, pl.ds(0, SUB), :], sems.at[0]),
        pltpu.make_async_copy(heat_ref, heat_hbm, sems.at[1]),
    ]
    for copy in copies:
        copy.start()
    for copy in copies:
        copy.wait()


def interval(
    sizes,
    thermal_anomaly,
    right_face_transport_ratio,
    species_ratios,
    lateral_spreading_number,
    depth_physics_operator,
    exchange_weight_table,
    sky_point_of_entry,
    water_indicator,
):
    sections, tile_count, lev_count = sizes
    _, levels, width = thermal_anomaly.shape
    tracers = species_ratios.shape[1]
    tiles = width // LANES
    rows = levels * tiles
    f32 = jnp.float32
    shape = jax.ShapeDtypeStruct
    flat = lambda x: x.reshape(rows, LANES)
    t, u, n = flat(thermal_anomaly), flat(right_face_transport_ratio), flat(lateral_spreading_number)
    q = jnp.transpose(species_ratios, (0, 2, 1, 3)).reshape(levels, tracers, width)
    lev = lax.axis_index("lev")

    group = 5 if levels % 5 == 0 else 1
    send_a, send_b, t_near, u_near, n_near, q_near = pl.pallas_call(
        functools.partial(edge_kernel, levels, tiles),
        out_shape=[shape((levels, LANES), f32)] * 2 + [shape((rows, LANES), f32)] * 3 + [shape((SUB, width), f32)],
        in_specs=[HBM] * 4,
        out_specs=[VMEM] * 6,
        scratch_shapes=[pltpu.SemaphoreType.DMA((4,))],
        compiler_params=PARAMS,
        name="edges",
    )(*(pltpu.with_memory_space_constraint(x, pltpu.HBM) for x in (t, u, n, q)))
    swap_a = [(i, i ^ 1) for i in range(tile_count)]
    swap_b = [(i, (i + 1) % tile_count if i % 2 else (i - 1) % tile_count) for i in range(tile_count)]
    got_a = lax.ppermute(send_a, "tile", swap_a)
    got_b = lax.ppermute(send_b, "tile", swap_b)
    pack = pl.pallas_call(
        functools.partial(pack_kernel, levels, tiles, group),
        out_shape=[shape((tracers, LANES), f32)] * 2,
        in_specs=[HBM],
        out_specs=[VMEM, VMEM],
        scratch_shapes=[pltpu.VMEM((levels, tracers, LANES), f32)] * 2
        + [pltpu.SemaphoreType.DMA((2, levels // group))],
        compiler_params=PARAMS,
        name="pack",
    )
    side_a, side_b = pack(pltpu.with_memory_space_constraint(q, pltpu.HBM))
    got_side_a = lax.ppermute(side_a, "tile", swap_a)
    got_side_b = lax.ppermute(side_b, "tile", swap_b)

    heating = pl.pallas_call(
        functools.partial(heat_kernel, levels, tiles, sections),
        out_shape=[shape((rows, LANES), f32), shape((5, levels, width), f32), shape((SUB, width), f32)],
        in_specs=[VMEM] * 6,
        out_specs=[VMEM] * 3,
        compiler_params=PARAMS,
        name="heat",
    )
    heat, coef, top = heating(t_near, u_near, n_near, q_near, got_a, got_b)

    others = [
        lax.ppermute(heat, "lev", [(i, peer(i, s, lev_count)) for i in range(lev_count)])
        for s in range(1, lev_count)
    ]

    index = sky_point_of_entry.T
    first = ((index[0, 0:1] + REACH) % (tile_count * width)) // width * tiles
    estimate = pl.CostEstimate(
        flops=9 * levels * tracers * width, bytes_accessed=4 * levels * tracers * width, transcendentals=0
    )
    inside = pl.pallas_call(
        functools.partial(inner_kernel, levels, tiles, tile_count),
        out_shape=[
            shape((levels, tracers, width), f32),
            shape(index.shape, jnp.int32),
            shape(index.shape, jnp.int32),
        ],
        in_specs=[SMEM] + [VMEM] * 3,
        out_specs=[VMEM] * 3,
        cost_estimate=estimate,
        compiler_params=PARAMS,
        name="inside",
    )
    part, inner, outer = inside(first, q, coef, index)

    mine = lax.dynamic_slice_in_dim(depth_physics_operator[0], lev * levels, levels, 0)
    columns = [
        lax.dynamic_slice_in_dim(mine, source_of(lev, s, lev_count) * levels, levels, 1)
        for s in range(lev_count)
    ]
    matrix = jnp.concatenate(columns, axis=1)
    mixed, surface = pl.pallas_call(
        functools.partial(surface_kernel, levels, tiles, lev_count),
        out_shape=[shape((levels, width), f32), shape((tiles * NFLUX, LANES), f32)],
        in_specs=[VMEM] * (lev_count + 2),
        out_specs=[VMEM, VMEM],
        scratch_shapes=[pltpu.VMEM((levels * lev_count, width), f32)],
        compiler_params=PARAMS,
        name="surface",
    )(matrix, heat, *others, top)

    half = sections // 2
    place = lambda c, i, l: (c * tile_count + i) * lev_count + l

    def across(s):
        pairs = [
            (place(c, i, l), place((c + half) % sections, i ^ s, l))
            for c in range(sections)
            for i in range(tile_count)
            for l in range(lev_count)
        ]
        return lax.ppermute(surface, ("comp", "tile", "lev"), pairs)

    direct = [across(s) for s in range(1, tile_count, 2)]
    joined = jnp.concatenate(direct, axis=0)
    shared = lax.ppermute(joined, "tile", swap_a)

    finish = pl.pallas_call(
        functools.partial(outer_kernel, levels, tiles, group),
        out_shape=shape((levels, tracers, width), f32),
        in_specs=[VMEM] * 5,
        out_specs=HBM,
        scratch_shapes=[pltpu.VMEM((levels, tracers, width), f32), pltpu.SemaphoreType.DMA((levels // group,))],
        cost_estimate=estimate,
        compiler_params=PARAMS,
        name="finish",
    )
    moved = finish(part, coef, got_side_a, got_side_b, mixed)

    heat_out, q_out = pl.pallas_call(
        functools.partial(final_kernel, levels, tiles, tile_count, sections),
        out_shape=[shape((rows, LANES), f32), shape((levels, tracers, width), f32)],
        in_specs=[SMEM] + [VMEM] * 8 + [HBM],
        out_specs=[HBM, HBM],
        scratch_shapes=[
            pltpu.VMEM((tile_count * tiles * SUB, LANES), f32),
            pltpu.VMEM((SUB, width), f32),
            pltpu.VMEM((rows, LANES), f32),
            pltpu.SemaphoreType.DMA((2,)),
        ],
        input_output_aliases={9: 1},
        compiler_params=PARAMS,
        name="remap",
    )(
        first, inner, outer, mixed, top, exchange_weight_table.T, water_indicator.reshape(1, width), joined, shared, moved
    )
    thermal_anomaly_ending = heat_out.reshape(1, levels, width)
    species_ratios_ending = jnp.transpose(q_out.reshape(1, levels, tracers, width), (0, 2, 1, 3))
    return thermal_anomaly_ending, species_ratios_ending


def solution(mesh):
    in_specs = (
        P("comp", "lev", "tile"),
        P("comp", "lev", "tile"),
        P("comp", None, "lev", "tile"),
        P("comp", "lev", "tile"),
        P("comp", None, None),
        P("tile", None),
        P("tile", None),
        P("tile"),
    )
    out_specs = (P("comp", "lev", "tile"), P("comp", None, "lev", "tile"))
    sizes = (mesh.shape["comp"], mesh.shape["tile"], mesh.shape["lev"])
    return jax.shard_map(
        functools.partial(interval, sizes), mesh=mesh, in_specs=in_specs, out_specs=out_specs, check_vma=False
    )
```
